32 devices in a mesh: segment: 4 (over y, x), mp: 8 (over z, core).
Axes of the slice: x: 2, y: 2, z: 4, core: 2. Of those that a mesh axis runs over, the one named last changes fastest.
Arguments:
- noise_init: float32 [2048, 64], P('segment'), may hold values from -6 to 6
- step_noise: float32 [4, 2048, 64], P(None, 'segment'), may hold values from -6 to 6
- assign: int32 [32], P('segment'), may hold values from 0 to 7
- slot_map: int32 [32], replicated, may hold values from 0 to 63, as said below
- prompt_embed: bfloat16 [8, 1536], P('segment', 'mp'), may hold values from -6 to 6
- time_vec: bfloat16 [1536], P('mp'), may hold values from -6 to 6
- w_in: bfloat16 [64, 1536], P('segment', 'mp'), may hold values from -0.75 to 0.75
- ln_gain: bfloat16 [1536], P('mp'), may hold values from 0.099609375 to 1.8984375
- w_up: bfloat16 [1536, 6144], P('segment', 'mp'), may hold values from -0.15625 to 0.15625
- w_down: bfloat16 [6144, 1536], P('mp', 'segment'), may hold values from -0.109375 to 0.109375
- w_out: bfloat16 [1536, 64], P('mp', 'segment'), may hold values from -0.15625 to 0.15625
- conv_in_w: bfloat16 [3, 3, 16, 512], replicated, may hold values from -0.5 to 0.5
- gn_gain: float32 [512], replicated, may hold values from 0.1 to 1.9
- conv_mid_w: bfloat16 [3, 3, 512, 512], replicated, may hold values from -0.09375 to 0.09375
Outputs:
- latents: float32 [2048, 64], P('segment')
- decoded: bfloat16 [64, 2, 128, 512], P('segment', None, 'mp')
The draws below stay inside these ranges and needn't reach their ends.
Inputs may be any that keep to these rules, and one draw needn't show every extreme that they name: `slot_map`: different samples have different slots. Decoder section d owns slots d * 16 to (d + 1) * 16 - 1; in every draw some section has all of its 16 slots filled, and slots 0 and 63 are used.
All inputs are finite; a program needn't handle non-finite values.
Results may differ from the reference program's by a relative error of at most 0.015.
Values may be sent and summed in bfloat16 or wider, within the bound.
No kernel may reach another device: no remote copies, remote signals or barrier semaphores. Data moves between devices by JAX's collectives and lax.ppermute only.
A program may use at most 64 MiB of HBM per device.

```python
import jax
import jax.numpy as jnp
from jax import lax

D = 1536
FF = 6144
LAT_CH = 16
VC = 512
GROUPS = 32
LCOLS = 128
STEPS = 4
PCH = 64
TOK_SAMPLE = 64
DSLOT = 16
SAMPLES = 32
TOKENS = 2048
SLOTS = 64
PROMPTS = 8
N_MP = 8


def draw_slot_map(key, part):
    section_key = jax.random.fold_in(key, 101)
    order_key = jax.random.fold_in(key, 202)
    sample_key = jax.random.fold_in(key, 303)
    sections = SLOTS // DSLOT
    chosen_section = jax.random.randint(section_key, (), 0, sections).astype(jnp.int32)
    shuffled = jax.random.permutation(order_key, SLOTS).astype(jnp.int32)
    positions = jnp.arange(SLOTS, dtype=jnp.int32)
    forced = (positions // DSLOT == chosen_section) | (positions == 0) | (positions == SLOTS - 1)
    scores = shuffled - SLOTS * forced.astype(jnp.int32)
    ordering = jnp.argsort(scores, stable=True).astype(jnp.int32)
    chosen = ordering[:SAMPLES]
    mixing = jax.random.permutation(sample_key, SAMPLES).astype(jnp.int32)
    return chosen[mixing].astype(jnp.int32)


def plant(drawn, key, smallest, largest):
    spot = [jax.random.randint(jax.random.fold_in(key, axis), (), 0, length) for axis, length in enumerate(drawn.shape)]
    longest = drawn.shape.index(max(drawn.shape))
    beside = spot[:longest] + [(spot[longest] + 1) % drawn.shape[longest]] + spot[longest + 1:]
    return drawn.at[tuple(spot)].set(smallest).at[tuple(beside)].set(largest)


def with_spikes(values, rng, source, target, shards_of, factor):
    def block_of(position):
        return (jnp.arange(values.shape[position]) // (values.shape[position] // shards_of)).reshape((-1,) + (1,) * (values.ndim - 1 - position))

    first = jax.random.permutation(rng, shards_of)[block_of(target)]
    other_side = (block_of(target) + shards_of // 2) % shards_of
    return jnp.where((block_of(source) == first) | (block_of(source) == other_side), factor * values, values)


def block_scale(own_key, shape, cuts, smallest, largest):
    factor_of, own = 1.0, jax.random.fold_in(own_key, 6)
    for dim, blocks in cuts:
        steps = jnp.exp(jax.random.uniform(jax.random.fold_in(own, dim), (blocks,), jnp.float32, smallest / len(cuts), largest / len(cuts)))
        factor_of = factor_of * jnp.repeat(steps, shape[dim] // blocks).reshape([-1 if axis == dim else 1 for axis in range(len(shape))])
    return factor_of


def scatter_about(rng, dims, scale, reach, cuts=(), kind=jnp.bfloat16):
    gain = block_scale(rng, dims, cuts, -0.22, 0.18) if cuts else 1.0
    array = jax.random.normal(rng, dims, jnp.float32) * scale * gain
    return jnp.minimum(jnp.maximum(array, -reach), reach).astype(kind)


def heavy_noise(own_key, extent, deviation, limit, cuts, heavy, kind=jnp.bfloat16):
    array = deviation * jax.random.normal(own_key, extent, jnp.float32)
    if cuts:
        array = array * block_scale(own_key, extent, cuts, -0.22, 0.18)
    return jnp.clip(with_spikes(array, jax.random.fold_in(own_key, 3), *heavy), -limit, limit).astype(kind)


def setup_inputs(seed: int = 0) -> dict:
    seeds = jax.random.split(jax.random.key(seed), 15)
    return {
        "noise_init": scatter_about(seeds[0], (TOKENS, PCH), 1.0, 6.0, ((0, 4),), jnp.float32),
        "step_noise": scatter_about(seeds[1], (STEPS, TOKENS, PCH), 1.0, 6.0, ((1, 4),), jnp.float32),
        "assign": plant(jax.random.randint(seeds[2], (SAMPLES,), 0, PROMPTS), jax.random.fold_in(seeds[2], 1), 0, PROMPTS - 1).astype(jnp.int32),
        "slot_map": draw_slot_map(jax.random.fold_in(seeds[14], 71), 0),
        "prompt_embed": scatter_about(seeds[4], (PROMPTS, D), 1.0, 6.0, ((0, 4), (1, 8))),
        "time_vec": scatter_about(seeds[5], (D,), 1.0, 6.0, ((0, 8),)),
        "w_in": scatter_about(seeds[6], (PCH, D), PCH ** -0.5, 0.75, ((0, 4), (1, 8))),
        "ln_gain": jnp.clip(1.0 + 0.18 * jax.random.normal(seeds[7], (D,), jnp.float32), 0.099609375, 1.8984375).astype(jnp.bfloat16),
        "w_up": scatter_about(seeds[8], (D, FF), D ** -0.5, 0.15625, ((0, 4), (1, 8))),
        "w_down": heavy_noise(seeds[9], (FF, D), FF ** -0.5, 0.109375, ((0, 8), (1, 4)), (0, 1, 8, 2.0)),
        "w_out": scatter_about(seeds[10], (D, PCH), D ** -0.5, 0.15625, ((0, 8), (1, 4))),
        "conv_in_w": scatter_about(seeds[11], (3, 3, LAT_CH, VC), (9 * LAT_CH) ** -0.5, 0.5),
        "gn_gain": jnp.clip(1.0 + 0.18 * jax.random.normal(seeds[12], (VC,), jnp.float32), 0.1, 1.9),
        "conv_mid_w": scatter_about(seeds[13], (3, 3, VC, VC), (9 * VC) ** -0.5, 0.09375),
    }


NOISE_SCALE = 0.5
LATENT_SCALE = 1.0 / 1.5305
EPSILON = 1e-06

def conv_three(padded, weight, col_count):
    accumulated = jnp.zeros((2, col_count, weight.shape[3]), jnp.float32)
    for row_shift in range(3):
        for col_shift in range(3):
            window = padded[row_shift:row_shift + 2, col_shift:col_shift + col_count, :]
            accumulated = accumulated + jnp.dot(window.reshape(2 * col_count, -1), weight[row_shift, col_shift], preferred_element_type=jnp.float32).reshape(2, col_count, -1)
    return accumulated

def reference(noise_init, step_noise, assign, slot_map, prompt_embed, time_vec, w_in, ln_gain, w_up, w_down, w_out, conv_in_w, gn_gain, conv_mid_w):
    prompt_cond = jnp.repeat(prompt_embed.astype(jnp.float32)[assign], TOK_SAMPLE, axis=0)
    latent_state = noise_init
    step_size = 1.0 / STEPS
    block_width = FF // N_MP
    for step_index in range(STEPS):
        time_now = 1.0 - step_index * step_size
        hidden_in = jnp.dot(latent_state.astype(jnp.bfloat16), w_in, preferred_element_type=jnp.float32) + prompt_cond + time_now * time_vec.astype(jnp.float32)
        average = lax.optimization_barrier(jnp.mean(hidden_in, axis=-1, keepdims=True))
        centered = hidden_in - average
        variance = lax.optimization_barrier(jnp.mean(centered * centered, axis=-1, keepdims=True))
        normed = (centered * lax.rsqrt(variance + EPSILON) * ln_gain.astype(jnp.float32)).astype(jnp.bfloat16)
        act = jax.nn.gelu(jnp.dot(normed, w_up, preferred_element_type=jnp.float32), approximate=True).astype(jnp.bfloat16)
        mlp_out = jnp.zeros(hidden_in.shape, jnp.float32)
        for block_index in range(N_MP):
            partial_value = jnp.dot(act[:, block_index * block_width:(block_index + 1) * block_width], w_down[block_index * block_width:(block_index + 1) * block_width], preferred_element_type=jnp.float32)
            rounded = lax.optimization_barrier(partial_value.astype(jnp.bfloat16))
            mlp_out = mlp_out + rounded.astype(jnp.float32)
        velocity = jnp.dot((hidden_in + mlp_out).astype(jnp.bfloat16), w_out, preferred_element_type=jnp.float32)
        latent_state = latent_state - step_size * velocity + NOISE_SCALE * jnp.sqrt(step_size) * step_noise[step_index]
    latents = latent_state
    images = latent_state.reshape(SAMPLES, TOK_SAMPLE, 2, 2, LAT_CH).transpose(0, 2, 1, 3, 4).reshape(SAMPLES, 2, LCOLS, LAT_CH)
    slot_in = jnp.zeros((SLOTS, 2, LCOLS, LAT_CH), jnp.float32).at[slot_map].set(images * LATENT_SCALE)
    per_group = VC // GROUPS

    def decode_one(latent_img):
        padded = jnp.pad(latent_img.astype(jnp.bfloat16), ((1, 1), (1, 1), (0, 0)))
        conv_first = conv_three(padded, conv_in_w, LCOLS)
        grouped = conv_first.reshape(2 * LCOLS, GROUPS, per_group)
        average = lax.optimization_barrier(jnp.mean(grouped, axis=(0, 2)))
        centered = grouped - average[None, :, None]
        variance = lax.optimization_barrier(jnp.mean(centered * centered, axis=(0, 2)))
        normed = (centered * lax.rsqrt(variance + EPSILON)[None, :, None]).reshape(2, LCOLS, VC) * gn_gain
        activated = jax.nn.silu(normed).astype(jnp.bfloat16)
        padded_act = jnp.pad(activated, ((1, 1), (1, 1), (0, 0)))
        return (conv_first + conv_three(padded_act, conv_mid_w, LCOLS)).astype(jnp.bfloat16)
    decoded = lax.map(decode_one, slot_in)
    return (latents, decoded)
```

```python
import functools
import math

import jax
import jax.numpy as jnp
from jax import lax
from jax.experimental import pallas as pl
from jax.experimental.pallas import tpu as pltpu
from jax.sharding import PartitionSpec as P

LAT_CH = 16
VC = 512
GROUPS = 32
STEPS = 4


NOISE_SCALE = 0.5
LATENT_SCALE = 1.0 / 1.5305
EPSILON = 1e-06
GELU_A = math.sqrt(2.0 / math.pi)
GELU_B = GELU_A * 0.044715


def with_halo(cells, sides, width):
    for axis, dim in sides:
        count = lax.axis_size(axis)
        ends = count - 1
        head = lax.slice_in_dim(cells, 0, width, axis=dim)
        tail = lax.slice_in_dim(cells, cells.shape[dim] - width, cells.shape[dim], axis=dim)
        cells = jnp.concatenate(
            [
                lax.ppermute(tail, axis, [(i, (i + 1) % count) for i in range(ends)]),
                cells,
                lax.ppermute(head, axis, [((i + 1) % count, i) for i in range(ends)]),
            ],
            axis=dim,
        )
    return cells


def conv_rows(padded, weight, col_count):
    accumulated = None
    for row_shift in range(3):
        for col_shift in range(3):
            window = padded[:, row_shift : row_shift + 2, col_shift : col_shift + col_count, :]
            product = jnp.einsum(
                "nrcv,vw->nrcw",
                window,
                weight[row_shift, col_shift],
                preferred_element_type=jnp.float32,
            )
            accumulated = product if accumulated is None else accumulated + product
    return accumulated


def decode_tile(latent_tile, tile_cols, image_cols, conv_in_w, gn_gain, conv_mid_w):
    slot_rows = latent_tile.shape[0]
    padded = jnp.pad(latent_tile.astype(jnp.bfloat16), ((0, 0), (1, 1), (0, 0), (0, 0)))
    first_wide = conv_rows(padded, conv_in_w, tile_cols + 2)
    conv_first = first_wide[:, :, 1 : tile_cols + 1, :]
    per_group = VC // GROUPS
    grouped = conv_first.reshape(slot_rows, 2 * tile_cols, GROUPS, per_group)
    group_sum, group_square = lax.psum(
        (jnp.sum(grouped, axis=(1, 3)), jnp.sum(grouped * grouped, axis=(1, 3))), "mp"
    )
    entries = 2 * image_cols * per_group
    average = group_sum / entries
    variance = jnp.maximum(group_square / entries - average * average, 0.0)
    inv_spread = lax.rsqrt(variance + EPSILON)
    col_count = conv_first.shape[2]
    shaped = conv_first.reshape(slot_rows, 2, col_count, GROUPS, per_group)
    shaped = (shaped - average[:, None, None, :, None]) * inv_spread[:, None, None, :, None]
    activated = jax.nn.silu(shaped.reshape(slot_rows, 2, col_count, VC) * gn_gain).astype(
        jnp.bfloat16
    )
    act_wide = with_halo(activated, (("mp", 2),), 1)
    act_padded = jnp.pad(act_wide, ((0, 0), (1, 1), (0, 0), (0, 0)))
    return (conv_first + conv_rows(act_padded, conv_mid_w, tile_cols)).astype(jnp.bfloat16)


def full_front(
    latent_state,
    w_in_full,
    prompt_cond,
    time_full,
    gain_full,
    time_now,
    samples_here,
    tok_sample,
    tok_group,
):
    embedded = jnp.dot(
        latent_state.astype(jnp.bfloat16), w_in_full, preferred_element_type=jnp.float32
    )
    hidden_in = (embedded.reshape(samples_here, tok_sample, -1) + prompt_cond[:, None, :]).reshape(
        tok_group, -1
    ) + time_now * time_full.astype(jnp.float32)
    average = jnp.mean(hidden_in, axis=-1, keepdims=True)
    centered = hidden_in - average
    variance = jnp.mean(centered * centered, axis=-1, keepdims=True)
    normed = (centered * lax.rsqrt(variance + EPSILON) * gain_full.astype(jnp.float32)).astype(
        jnp.bfloat16
    )
    return (hidden_in, normed)


def per_device(
    noise_init,
    step_noise,
    assign,
    slot_map,
    prompt_embed,
    time_vec,
    w_in,
    ln_gain,
    w_up,
    w_down,
    w_out,
    conv_in_w,
    gn_gain,
    conv_mid_w,
):
    mp_count = lax.axis_size("mp")
    mp_index = lax.axis_index("mp")
    segment_index = lax.axis_index("segment")
    w_in_rows, w_up_rows, w_down_cols, w_out_cols, prompt_rows = (
        lax.all_gather(w_in, "segment", axis=0, tiled=True),
        lax.all_gather(w_up, "segment", axis=0, tiled=True),
        lax.all_gather(w_down, "segment", axis=1, tiled=True),
        lax.all_gather(w_out, "segment", axis=1, tiled=True),
        lax.all_gather(prompt_embed, "segment", axis=0, tiled=True),
    )
    samples_here = assign.shape[0]
    tok_group = noise_init.shape[0]
    tok_sample = tok_group // samples_here
    prompt_count = prompt_rows.shape[0]
    choose = (assign[:, None] == jnp.arange(prompt_count, dtype=jnp.int32)[None, :]).astype(
        jnp.bfloat16
    )
    step_size = 1.0 / STEPS
    noise_gain = NOISE_SCALE * math.sqrt(step_size)
    latent_state = noise_init
    w_in_full, prompt_full, w_out_full, time_full, gain_full = (
        lax.all_gather(w_in_rows, "mp", axis=1, tiled=True),
        lax.all_gather(prompt_rows, "mp", axis=1, tiled=True),
        lax.all_gather(w_out_cols, "mp", axis=0, tiled=True),
        lax.all_gather(time_vec, "mp", axis=0, tiled=True),
        lax.all_gather(ln_gain, "mp", axis=0, tiled=True),
    )
    prompt_cond = jnp.dot(choose, prompt_full, preferred_element_type=jnp.float32)
    for step_index in range(STEPS):
        time_now = 1.0 - step_index * step_size
        hidden_in, normed = full_front(
            latent_state,
            w_in_full,
            prompt_cond,
            time_full,
            gain_full,
            time_now,
            samples_here,
            tok_sample,
            tok_group,
        )
        act = jax.nn.gelu(
            jnp.dot(normed, w_up_rows, preferred_element_type=jnp.float32), approximate=True
        ).astype(jnp.bfloat16)
        mlp_out = lax.psum(
            jnp.dot(act, w_down_cols, preferred_element_type=jnp.float32).astype(jnp.bfloat16), "mp"
        ).astype(jnp.float32)
        velocity = jnp.dot(
            (hidden_in + mlp_out).astype(jnp.bfloat16),
            w_out_full,
            preferred_element_type=jnp.float32,
        )
        latent_state = latent_state - step_size * velocity + noise_gain * step_noise[step_index]
    image_cols = 2 * tok_sample
    tile_cols = image_cols // mp_count
    images = (
        latent_state.reshape(samples_here, tok_sample, 2, 2, LAT_CH)
        .transpose(0, 2, 1, 3, 4)
        .reshape(samples_here, 2, image_cols, LAT_CH)
        * LATENT_SCALE
    )
    widened = jnp.pad(images, ((0, 0), (0, 0), (2, 2), (0, 0)))
    latent_tile = lax.dynamic_slice_in_dim(widened, mp_index * tile_cols, tile_cols + 4, 2)
    slot_count = 2 * samples_here
    first_slot = segment_index * slot_count
    slot_ids = first_slot + jnp.arange(slot_count, dtype=jnp.int32)
    slot_picks = (slot_map[None, :] == slot_ids[:, None]).astype(jnp.float32)
    flat_tile = latent_tile.reshape(samples_here, -1)
    owned = jnp.dot(
        slot_picks,
        lax.all_gather(flat_tile, "segment", axis=0, tiled=True),
        preferred_element_type=jnp.float32,
        precision=lax.Precision.HIGHEST,
    )
    decoded = decode_tile(
        owned.reshape(slot_count, 2, tile_cols + 4, LAT_CH),
        tile_cols,
        image_cols,
        conv_in_w,
        gn_gain,
        conv_mid_w,
    )
    return (latent_state, decoded)


ROWS = 40
PIECE = 128


def xor_pieces(value, axis, masks):
    count = lax.axis_size(axis)
    return [
        lax.ppermute(value, axis, [(i, i ^ mask) for i in range(count)]) for mask in masks
    ]


def split_three(value):
    high = value.astype(jnp.bfloat16)
    rest = value - high.astype(jnp.float32)
    middle = rest.astype(jnp.bfloat16)
    low = (rest - middle.astype(jnp.float32)).astype(jnp.bfloat16)
    return high, middle, low


def dot32(left, right):
    return jnp.dot(left, right, preferred_element_type=jnp.float32)


def dot_exact(value, exact):
    high, middle, low = split_three(value)
    return dot32(high, exact) + dot32(middle, exact) + dot32(low, exact)


def whole(shape_count):
    return [pl.BlockSpec(memory_space=pltpu.VMEM)] * shape_count


def split_kernel(segments, quarter, w_up_ref, w_down_ref, *outs):
    mine = lax.axis_index("segment")
    rows = w_up_ref.shape[0]
    half = rows // 2
    for other in range(segments):
        up_ref, down_ref = outs[other], outs[segments + other]
        target = lax.bitwise_xor(mine, other)
        start = pl.multiple_of(target * quarter, quarter)
        down_ref[...] = w_down_ref[pl.ds(start, quarter), :]
        for part in range(segments):

            @pl.when(target == part)
            def _():
                block = w_up_ref[:, part * quarter : (part + 1) * quarter]
                up_ref[0:rows, :] = block[:, 0:128]
                tail = block[:, 128:quarter]
                up_ref[rows : rows + half, 0:64] = tail[0:half]
                up_ref[rows : rows + half, 64:128] = tail[half:rows]


def prep_kernel(cfg, *refs):
    segments, features, slices, latent, prompts = cfg
    own_ref, other_ref = refs[0], refs[1]
    ups = refs[2 : 2 + segments]
    downs = refs[2 + segments : 2 + 2 * segments]
    piece_ref, extra_ref, table_ref, w_out_ref, canon = refs[2 + 2 * segments :]
    seg = lax.axis_index("segment")
    mp = lax.axis_index("mp")
    width = own_ref.shape[2]
    stack = own_ref.shape[1]
    in_rows = latent // segments
    prompt_rows = prompts // segments
    column = lax.broadcasted_iota(jnp.int32, (256, stack), 1)
    block = jnp.zeros_like(column)
    for edge in range(1, segments):
        block = block + (column >= edge * ROWS).astype(jnp.int32)
    inner = column - block * ROWS
    source = lax.bitwise_xor(block, seg)
    target = jnp.where(
        inner < in_rows,
        source * in_rows + inner,
        jnp.where(
            inner < 2 * in_rows,
            192 + source * in_rows + inner - in_rows,
            jnp.where(
                inner < 2 * in_rows + prompt_rows,
                64 + source * prompt_rows + inner - 2 * in_rows,
                jnp.where(
                    (block == 0) & (inner < 2 * in_rows + prompt_rows + 2),
                    64 + prompts + inner - 2 * in_rows - prompt_rows,
                    1000,
                ),
            ),
        ),
    )
    row = lax.broadcasted_iota(jnp.int32, (256, stack), 0)
    place = (row == target).astype(jnp.float32).astype(jnp.bfloat16)
    total = jnp.zeros((128, 1), jnp.float32)
    for index in range(slices):
        ref = own_ref if index % 2 == 0 else other_ref
        where_to = lax.bitwise_xor(mp, index)
        both = dot32(place, ref[index // 2])
        canon[where_to] = both[0:128]
        table_ref[where_to] = both[0:80].astype(jnp.bfloat16)
        start = pl.multiple_of(where_to * width, width)
        w_out_ref[pl.ds(start, width), :] = jnp.transpose(both[128:256]).astype(jnp.bfloat16)
        total = total + jnp.sum(both[0:128], axis=1, keepdims=True)
    average = total / features
    per_segment = slices // segments
    main = jnp.zeros((128, 128), jnp.float32)
    tail = jnp.zeros((128, 128), jnp.float32)
    down = jnp.zeros((downs[0].shape[0], 128), jnp.float32)
    for other in range(segments):
        source_seg = lax.bitwise_xor(seg, other)
        rows = per_segment * width
        for unit in range(per_segment):
            where_from = source_seg * per_segment + unit
            part = canon[where_from]
            gain = canon[where_from, 64 + prompts + 1 : 64 + prompts + 2, :]
            scaled = (part - average) * gain
            high = scaled.astype(jnp.bfloat16)
            low = (scaled - high.astype(jnp.float32)).astype(jnp.bfloat16)
            both = jnp.concatenate([high, low], axis=0)
            product = dot32(both, ups[other][unit * width : (unit + 1) * width, :])
            main = main + product[0:128] + product[128:256]
            product = dot32(both, ups[other][rows : rows + rows // 2, :])
            product = product[0:128] + product[128:256]
            tail = tail + (product if unit == 0 else pltpu.roll(product, 64, 1))
        start = pl.multiple_of(source_seg * rows, rows)
        down = down + dot32(downs[other][...], w_out_ref[pl.ds(start, rows), :])
    lane = lax.broadcasted_iota(jnp.int32, (1, 128), 1)
    down = 0.5 * down
    piece_ref[0:128, :] = jnp.where(lane < 64, jnp.transpose(main), down[0:128]).astype(
        jnp.bfloat16
    )
    piece_ref[128:192, :] = jnp.where(
        lane < 64, jnp.transpose(tail)[0:64], down[128:192]
    ).astype(jnp.bfloat16)
    extra_ref[0:16, :] = main[64:80].astype(jnp.bfloat16)
    extra_ref[16:32, :] = tail[64:80].astype(jnp.bfloat16)


def loop_kernel(cfg, *refs):
    features, slices, prompts, pieces = cfg
    (assign_ref, noise_ref, step_ref, table_ref, w_out_ref, w_a, w_b, latents_ref, patch_ref,
     state, steps, const_a, const_b, hidden) = refs
    mp = lax.axis_index("mp")
    tokens = latents_ref.shape[0]
    width = table_ref.shape[2]
    start = pl.multiple_of(mp * tokens, tokens)
    prompt = assign_ref[mp]
    lane = lax.broadcasted_iota(jnp.int32, (1, 128), 1)
    state[...] = jnp.zeros_like(state)
    state[:, 0:64] = noise_ref[pl.ds(start, tokens), :]
    steps[...] = jnp.zeros_like(steps)
    steps[:, :, 0:64] = step_ref[:, pl.ds(start, tokens), :]
    sixteen = lax.broadcasted_iota(jnp.int32, (16, 1), 0)
    pick = (sixteen == prompt).astype(jnp.float32)
    timing = (sixteen == prompts).astype(jnp.float32)
    main_rows = pieces * 192
    for w_ref, const in ((w_a, const_a), (w_b, const_b)):
        for block in range(w_ref.shape[0]):
            for pair in range(pieces // 2):
                base = main_rows + pair * 64
                e = [
                    w_ref[block, base + 16 * i : base + 16 * i + 16, :].astype(jnp.float32)
                    for i in range(4)
                ]
                turned = pltpu.roll(e[2], 64, 1)
                lanes = [
                    e[0],
                    jnp.where(lane < 64, e[1], turned),
                    jnp.where(lane < 64, turned, pltpu.roll(e[3], 64, 1)),
                ]
                for third in range(3):
                    at = pair * 384 + third * 128
                    const[block, 0:1, at : at + 128] = jnp.sum(
                        pick * lanes[third], axis=0, keepdims=True
                    )
                    const[block, 1:2, at : at + 128] = jnp.sum(
                        timing * lanes[third], axis=0, keepdims=True
                    )
    step_size = 1.0 / STEPS
    noise_gain = NOISE_SCALE * math.sqrt(step_size)

    def one_step(step, carry):
        time_now = 1.0 - step.astype(jnp.float32) * step_size
        now = state[...]
        operand = now.astype(jnp.bfloat16)
        narrow = operand[:, 0:64]
        weight = pick + time_now * timing
        total = jnp.zeros((tokens, 1), jnp.float32)
        for index in range(slices):
            base = jnp.sum(
                table_ref[index, 64:80, :].astype(jnp.float32) * weight, axis=0, keepdims=True
            )
            value = dot32(narrow, table_ref[index, 0:64, :]) + base
            hidden[index] = value
            total = total + jnp.sum(value, axis=1, keepdims=True)
        average = total / features
        square = jnp.zeros((tokens, 1), jnp.float32)
        velocity = jnp.zeros((tokens, 128), jnp.float32)
        for index in range(slices):
            value = hidden[index]
            centered = value - average
            square = square + jnp.sum(centered * centered, axis=1, keepdims=True)
            velocity = velocity + dot32(
                value.astype(jnp.bfloat16), w_out_ref[index * width : (index + 1) * width, :]
            )
        spread = lax.rsqrt(square / features + EPSILON)
        for w_ref, const in ((w_a, const_a), (w_b, const_b)):
            for block in range(w_ref.shape[0]):
                for at in range(0, main_rows, 384):
                    weights = w_ref[block, at : at + 384, :]
                    shift = (
                        const[block, 0:1, at : at + 384]
                        + time_now * const[block, 1:2, at : at + 384]
                    )
                    pre = lax.dot_general(
                        operand, weights, (((1,), (1,)), ((), ())),
                        preferred_element_type=jnp.float32,
                    )
                    pre = (pre + shift) * spread
                    inner = pre * (GELU_A + GELU_B * (pre * pre))
                    act = (pre + pre * jnp.tanh(inner)).astype(jnp.bfloat16)
                    velocity = velocity + dot32(act, weights)
        moved = pltpu.roll(velocity, 64, 1)
        fresh = now - step_size * moved + noise_gain * steps[step]
        state[...] = jnp.where(lane < 64, fresh, 0.0)
        return carry

    lax.fori_loop(0, STEPS, one_step, 0)
    final = state[...]
    latents_ref[...] = final[:, 0:64]
    image = final * LATENT_SCALE
    row = lax.broadcasted_iota(jnp.int32, (tokens, 128), 0)
    before = jnp.where(row == 0, 0.0, pltpu.roll(image, 1, 0))
    after = jnp.where(row == tokens - 1, 0.0, pltpu.roll(image, tokens - 1, 0))
    odd = lax.bitwise_and(lax.shift_right_logical(lane, 4), 1) == 1
    beside = pltpu.roll(jnp.where(odd, before, after), 64, 1)
    patch_ref[...] = (image + beside).astype(jnp.bfloat16)


def decode_kernel(cfg, *refs):
    segments, mp_count, samples_here, image_cols = cfg
    (map_ref, own_ref, other_ref, conv_in_ref, gain_ref, conv_mid_ref, out_ref, table, patches,
     front, sums, squares, means, act, center) = refs
    seg = lax.axis_index("segment")
    mp = lax.axis_index("mp")
    slots = out_ref.shape[0]
    half_pieces = own_ref.shape[0]
    pieces = 2 * half_pieces
    tokens = own_ref.shape[1]
    tile = out_ref.shape[2]
    tile_tokens = tile // 2
    lats = LAT_CH
    for slot in range(slots):
        table[slot] = pieces
    z_count = mp_count // 2
    for sample in range(map_ref.shape[0]):
        owner = lax.bitwise_xor(mp, sample % samples_here)
        place = (
            lax.bitwise_and(owner, 1) * half_pieces
            + lax.bitwise_xor(seg, sample // samples_here) * z_count
            + lax.shift_right_logical(owner, 1)
        )
        relative = map_ref[sample] - seg * slots

        @pl.when((relative >= 0) & (relative < slots))
        def _():
            table[relative] = place

    patches[0:half_pieces] = own_ref[...]
    patches[half_pieces:pieces] = other_ref[...]
    patches[pieces] = jnp.zeros_like(own_ref[0])
    front[...] = jnp.zeros_like(front)
    for group in range(8):
        if group < 4:
            row_in, offset = group // 2, group % 2
        else:
            row_in, offset = (group - 4) // 2, 2 if group % 2 == 0 else -1
        for out in range(4):
            row_out, col_out = out // 2, out % 2
            i, j = row_in - row_out + 1, offset - col_out + 1
            if 0 <= j <= 2:
                front[group * lats : (group + 1) * lats, out * VC : (out + 1) * VC] = (
                    conv_in_ref[i, j]
                )
    for slot in range(slots):
        patch = patches[table[slot]].astype(jnp.float32)
        sums[slot : slot + 1, :] = jnp.sum(patch, axis=0, keepdims=True)
    per_group = VC // GROUPS
    entries = 2 * image_cols * per_group
    row_c = lax.broadcasted_iota(jnp.int32, (VC, VC), 0) // per_group
    col_c = lax.broadcasted_iota(jnp.int32, (VC, VC), 1) // per_group
    same = (row_c == col_c).astype(jnp.float32).astype(jnp.bfloat16)
    wide = dot_exact(sums[...], front[...])
    wide = wide[:, 0:VC] + wide[:, VC : 2 * VC] + wide[:, 2 * VC : 3 * VC] + wide[:, 3 * VC :]
    average = dot_exact(wide, same) / entries
    means[...] = average

    def one_slot(slot, carry):
        patch = patches[table[slot]]
        mean = means[pl.ds(slot, 1), :]
        collected = None
        for out in range(4):
            value = dot32(patch, front[:, out * VC : (out + 1) * VC]) - mean
            value = value * value
            part = value[0:8]
            for at in range(8, tokens, 8):
                part = part + value[at : at + 8]
            collected = part if collected is None else collected + part
        squares[pl.ds(slot, 1), :] = jnp.sum(collected, axis=0, keepdims=True)
        return carry

    lax.fori_loop(0, slots, one_slot, 0)
    variance = dot_exact(squares[...], same) / entries
    spread = lax.rsqrt(variance + EPSILON)
    gain = gain_ref[...]
    count = (tile_tokens + 2) * slots
    row_t = lax.broadcasted_iota(jnp.int32, (count, 1), 0)
    token = row_t // slots
    slot_of = row_t - token * slots
    chosen = jnp.full((count, 1), pieces, jnp.int32)
    for slot in range(slots):
        chosen = jnp.where(slot_of == slot, table[slot], chosen)
    token = token + mp * tile_tokens - 1
    inside = (token >= 0) & (token < tokens)
    wanted = jnp.where(inside, chosen * tokens + token, -1)
    column = lax.broadcasted_iota(jnp.int32, (count, pieces * tokens), 1)
    pick = (column == wanted).astype(jnp.float32).astype(jnp.bfloat16)
    rows = dot32(pick, patches[0:pieces].reshape(pieces * tokens, 128)).astype(jnp.bfloat16)
    first_token = mp * tile_tokens - 1
    for out in range(4):
        row_out, col_out = out // 2, out % 2
        value = dot32(rows, front[:, out * VC : (out + 1) * VC])
        for t in range(tile_tokens + 2):
            part = value[t * slots : (t + 1) * slots]
            at = (2 * t + col_out) * slots
            if 1 <= t <= tile_tokens:
                center[row_out, at - 2 * slots : at - slots, :] = part
            scaled = (part - average) * spread * gain
            silu = 0.5 * scaled * (1.0 + jnp.tanh(0.5 * scaled))
            if t == 0:
                silu = jnp.where(mp == 0, 0.0, silu)
            if t == tile_tokens + 1:
                silu = jnp.where(mp == mp_count - 1, 0.0, silu)
            act[row_out, at : at + slots, :] = silu.astype(jnp.bfloat16)
    size = tile * slots
    row_p = lax.broadcasted_iota(jnp.int32, (size, size), 0)
    col_p = lax.broadcasted_iota(jnp.int32, (size, size), 1)
    slot_p = row_p // tile
    swap = (col_p == (row_p - slot_p * tile) * slots + slot_p).astype(jnp.float32)
    swap = swap.astype(jnp.bfloat16)
    for row_out in range(2):
        total = center[row_out]
        for row_in in range(2):
            for shift in range(3):
                at = (1 + shift) * slots
                total = total + dot32(
                    act[row_in, at : at + size, :], conv_mid_ref[row_in - row_out + 1, shift]
                )
        ordered = dot32(swap, total.astype(jnp.bfloat16)).astype(jnp.bfloat16)
        out_ref[:, row_out, :, :] = ordered.reshape(slots, tile, VC)


def order_kernel(own_ref, other_ref, out_ref):
    mp = lax.axis_index("mp")
    tokens = own_ref.shape[1]
    for index in range(2 * own_ref.shape[0]):
        ref = own_ref if index % 2 == 0 else other_ref
        start = pl.multiple_of(lax.bitwise_xor(mp, index) * tokens, tokens)
        out_ref[pl.ds(start, tokens), :] = ref[index // 2]


def per_device_fast(
    noise_init,
    step_noise,
    assign,
    slot_map,
    prompt_embed,
    time_vec,
    w_in,
    ln_gain,
    w_up,
    w_down,
    w_out,
    conv_in_w,
    gn_gain,
    conv_mid_w,
):
    segments = lax.axis_size("segment")
    mp_count = lax.axis_size("mp")
    around = range(1, segments)
    along = range(2, mp_count, 2)
    width = w_in.shape[1]
    features = width * mp_count
    latent = w_in.shape[0] * segments
    prompts = prompt_embed.shape[0] * segments
    samples_here = assign.shape[0]
    tok_group = noise_init.shape[0]
    tokens = tok_group // mp_count
    hidden = w_up.shape[1]
    quarter = hidden // segments
    bf16, f32 = jnp.bfloat16, jnp.float32
    used = 2 * w_in.shape[0] + prompt_embed.shape[0] + 2
    pack = jnp.concatenate(
        [
            w_in,
            w_out.T,
            prompt_embed,
            time_vec[None, :],
            ln_gain[None, :],
            jnp.zeros((ROWS - used, width), bf16),
        ],
        axis=0,
    )
    split = pl.pallas_call(
        functools.partial(split_kernel, segments, quarter),
        out_shape=[jax.ShapeDtypeStruct((w_up.shape[0] * 3 // 2, 128), bf16)] * segments
        + [jax.ShapeDtypeStruct((quarter, w_down.shape[1]), bf16)] * segments,
        in_specs=whole(2),
        out_specs=whole(2 * segments),
        name="split_weights",
    )(w_up, w_down)
    table = [pack] + xor_pieces(pack, "segment", around)
    ups, downs = [split[0]], [split[segments]]
    for other in around:
        ups += xor_pieces(split[other], "segment", [other])
        downs += xor_pieces(split[segments + other], "segment", [other])
    table = jnp.concatenate(table, axis=0)
    table = jnp.stack([table] + xor_pieces(table, "mp", along))
    (table_other,) = xor_pieces(table, "mp", [1])
    piece, extra, tables, w_out_all = pl.pallas_call(
        functools.partial(prep_kernel, (segments, features, mp_count, latent, prompts)),
        out_shape=[
            jax.ShapeDtypeStruct((quarter, 128), bf16),
            jax.ShapeDtypeStruct((32, 128), bf16),
            jax.ShapeDtypeStruct((mp_count, 80, width), bf16),
            jax.ShapeDtypeStruct((features, 128), bf16),
        ],
        in_specs=whole(2 + 2 * segments),
        out_specs=whole(4),
        scratch_shapes=[pltpu.VMEM((mp_count, 128, width), f32)],
        name="combine_weights",
    )(table, table_other, *ups, *downs)
    both = jnp.concatenate([piece, extra], axis=0)
    line = [both] + xor_pieces(both, "mp", along)
    line = jnp.concatenate([v[:quarter] for v in line] + [v[quarter:] for v in line], axis=0)
    plane = jnp.stack([line] + xor_pieces(line, "segment", around))
    (plane_other,) = xor_pieces(plane, "mp", [1])
    half = mp_count // 2
    const = pltpu.VMEM((segments, 8, half * quarter), f32)
    latents, patch = pl.pallas_call(
        functools.partial(loop_kernel, (features, mp_count, prompts, half)),
        out_shape=[
            jax.ShapeDtypeStruct((tokens, 64), f32),
            jax.ShapeDtypeStruct((tokens, 128), bf16),
        ],
        in_specs=[pl.BlockSpec(memory_space=pltpu.SMEM)] + whole(6),
        out_specs=whole(2),
        scratch_shapes=[
            pltpu.VMEM((tokens, 128), f32),
            pltpu.VMEM((STEPS, tokens, 128), f32),
            const,
            const,
            pltpu.VMEM((mp_count, tokens, width), f32),
        ],
        name="denoise",
    )(assign, noise_init, step_noise, tables, w_out_all, plane, plane_other)
    image = jnp.stack([patch] + xor_pieces(patch, "mp", along))
    image = jnp.concatenate([image] + xor_pieces(image, "segment", around), axis=0)
    (image_other,) = xor_pieces(image, "mp", [1])
    rows = jnp.stack([latents] + xor_pieces(latents, "mp", along))
    (rows_other,) = xor_pieces(rows, "mp", [1])
    latents_all = pl.pallas_call(
        order_kernel,
        out_shape=jax.ShapeDtypeStruct(noise_init.shape, f32),
        in_specs=whole(2),
        out_specs=whole(1)[0],
        name="order_latents",
    )(rows, rows_other)
    image_cols = 2 * tokens
    tile = image_cols // mp_count
    slots = 2 * samples_here
    pieces = segments * mp_count
    decoded = pl.pallas_call(
        functools.partial(decode_kernel, (segments, mp_count, samples_here, image_cols)),
        out_shape=jax.ShapeDtypeStruct((slots, 2, tile, VC), bf16),
        in_specs=[pl.BlockSpec(memory_space=pltpu.SMEM)] + whole(5),
        out_specs=whole(1)[0],
        scratch_shapes=[
            pltpu.SMEM((slots,), jnp.int32),
            pltpu.VMEM((pieces + 1, tokens, 128), bf16),
            pltpu.VMEM((128, 4 * VC), bf16),
            pltpu.VMEM((slots, 128), f32),
            pltpu.VMEM((slots, VC), f32),
            pltpu.VMEM((slots, VC), f32),
            pltpu.VMEM((2, (tile + 4) * slots, VC), bf16),
            pltpu.VMEM((2, tile * slots, VC), f32),
        ],
        name="decode",
    )(slot_map, image, image_other, conv_in_w, gn_gain[None, :], conv_mid_w)
    return latents_all, decoded


def suits(*shapes):
    segments, mp_count = lax.axis_size("segment"), lax.axis_size("mp")
    noise, assign, prompt, w_in, w_up = shapes
    return (
        mp_count == 2 * segments
        and noise[0] // mp_count == noise[0] // assign[0] == 64
        and w_up[1] // segments == w_in[1] == 192
        and w_in[0] * segments == noise[1] == 64
        and prompt[0] * segments <= 8
        and noise[0] == 64 * assign[0]
    )


def choose(*args):
    noise, assign, prompt, w_in, w_up = (args[i].shape for i in (0, 2, 4, 6, 8))
    ready = suits(noise, assign, prompt, w_in, w_up)
    return (per_device_fast if ready else per_device)(*args)


def solution(mesh):
    return jax.shard_map(
        choose,
        mesh=mesh,
        in_specs=(
            P("segment", None),
            P(None, "segment", None),
            P("segment"),
            P(),
            P("segment", "mp"),
            P("mp"),
            P("segment", "mp"),
            P("mp"),
            P("segment", "mp"),
            P("mp", "segment"),
            P("mp", "segment"),
            P(),
            P(),
            P(),
        ),
        out_specs=(P("segment", None), P("segment", None, "mp", None)),
        check_vma=False,
    )
```

```python
import functools
import math

import jax
import jax.numpy as jnp
from jax import lax
from jax.experimental import pallas as pl
from jax.experimental.pallas import tpu as pltpu
from jax.sharding import PartitionSpec as P

LAT_CH = 16
VC = 512
GROUPS = 32
STEPS = 4


NOISE_SCALE = 0.5
LATENT_SCALE = 1.0 / 1.5305
EPSILON = 1e-06
GELU_A = math.sqrt(2.0 / math.pi)
GELU_B = GELU_A * 0.044715


def with_halo(cells, sides, width):
    for axis, dim in sides:
        count = lax.axis_size(axis)
        ends = count - 1
        head = lax.slice_in_dim(cells, 0, width, axis=dim)
        tail = lax.slice_in_dim(cells, cells.shape[dim] - width, cells.shape[dim], axis=dim)
        cells = jnp.concatenate(
            [
                lax.ppermute(tail, axis, [(i, (i + 1) % count) for i in range(ends)]),
                cells,
                lax.ppermute(head, axis, [((i + 1) % count, i) for i in range(ends)]),
            ],
            axis=dim,
        )
    return cells


def conv_rows(padded, weight, col_count):
    accumulated = None
    for row_shift in range(3):
        for col_shift in range(3):
            window = padded[:, row_shift : row_shift + 2, col_shift : col_shift + col_count, :]
            product = jnp.einsum(
                "nrcv,vw->nrcw",
                window,
                weight[row_shift, col_shift],
                preferred_element_type=jnp.float32,
            )
            accumulated = product if accumulated is None else accumulated + product
    return accumulated


def decode_tile(latent_tile, tile_cols, image_cols, conv_in_w, gn_gain, conv_mid_w):
    slot_rows = latent_tile.shape[0]
    padded = jnp.pad(latent_tile.astype(jnp.bfloat16), ((0, 0), (1, 1), (0, 0), (0, 0)))
    first_wide = conv_rows(padded, conv_in_w, tile_cols + 2)
    conv_first = first_wide[:, :, 1 : tile_cols + 1, :]
    per_group = VC // GROUPS
    grouped = conv_first.reshape(slot_rows, 2 * tile_cols, GROUPS, per_group)
    group_sum, group_square = lax.psum(
        (jnp.sum(grouped, axis=(1, 3)), jnp.sum(grouped * grouped, axis=(1, 3))), "mp"
    )
    entries = 2 * image_cols * per_group
    average = group_sum / entries
    variance = jnp.maximum(group_square / entries - average * average, 0.0)
    inv_spread = lax.rsqrt(variance + EPSILON)
    col_count = conv_first.shape[2]
    shaped = conv_first.reshape(slot_rows, 2, col_count, GROUPS, per_group)
    shaped = (shaped - average[:, None, None, :, None]) * inv_spread[:, None, None, :, None]
    activated = jax.nn.silu(shaped.reshape(slot_rows, 2, col_count, VC) * gn_gain).astype(
        jnp.bfloat16
    )
    act_wide = with_halo(activated, (("mp", 2),), 1)
    act_padded = jnp.pad(act_wide, ((0, 0), (1, 1), (0, 0), (0, 0)))
    return (conv_first + conv_rows(act_padded, conv_mid_w, tile_cols)).astype(jnp.bfloat16)


def full_front(
    latent_state,
    w_in_full,
    prompt_cond,
    time_full,
    gain_full,
    time_now,
    samples_here,
    tok_sample,
    tok_group,
):
    embedded = jnp.dot(
        latent_state.astype(jnp.bfloat16), w_in_full, preferred_element_type=jnp.float32
    )
    hidden_in = (embedded.reshape(samples_here, tok_sample, -1) + prompt_cond[:, None, :]).reshape(
        tok_group, -1
    ) + time_now * time_full.astype(jnp.float32)
    average = jnp.mean(hidden_in, axis=-1, keepdims=True)
    centered = hidden_in - average
    variance = jnp.mean(centered * centered, axis=-1, keepdims=True)
    normed = (centered * lax.rsqrt(variance + EPSILON) * gain_full.astype(jnp.float32)).astype(
        jnp.bfloat16
    )
    return (hidden_in, normed)


def per_device(
    noise_init,
    step_noise,
    assign,
    slot_map,
    prompt_embed,
    time_vec,
    w_in,
    ln_gain,
    w_up,
    w_down,
    w_out,
    conv_in_w,
    gn_gain,
    conv_mid_w,
):
    mp_count = lax.axis_size("mp")
    mp_index = lax.axis_index("mp")
    segment_index = lax.axis_index("segment")
    w_in_rows, w_up_rows, w_down_cols, w_out_cols, prompt_rows = (
        lax.all_gather(w_in, "segment", axis=0, tiled=True),
        lax.all_gather(w_up, "segment", axis=0, tiled=True),
        lax.all_gather(w_down, "segment", axis=1, tiled=True),
        lax.all_gather(w_out, "segment", axis=1, tiled=True),
        lax.all_gather(prompt_embed, "segment", axis=0, tiled=True),
    )
    samples_here = assign.shape[0]
    tok_group = noise_init.shape[0]
    tok_sample = tok_group // samples_here
    prompt_count = prompt_rows.shape[0]
    choose = (assign[:, None] == jnp.arange(prompt_count, dtype=jnp.int32)[None, :]).astype(
        jnp.bfloat16
    )
    step_size = 1.0 / STEPS
    noise_gain = NOISE_SCALE * math.sqrt(step_size)
    latent_state = noise_init
    w_in_full, prompt_full, w_out_full, time_full, gain_full = (
        lax.all_gather(w_in_rows, "mp", axis=1, tiled=True),
        lax.all_gather(prompt_rows, "mp", axis=1, tiled=True),
        lax.all_gather(w_out_cols, "mp", axis=0, tiled=True),
        lax.all_gather(time_vec, "mp", axis=0, tiled=True),
        lax.all_gather(ln_gain, "mp", axis=0, tiled=True),
    )
    prompt_cond = jnp.dot(choose, prompt_full, preferred_element_type=jnp.float32)
    for step_index in range(STEPS):
        time_now = 1.0 - step_index * step_size
        hidden_in, normed = full_front(
            latent_state,
            w_in_full,
            prompt_cond,
            time_full,
            gain_full,
            time_now,
            samples_here,
            tok_sample,
            tok_group,
        )
        act = jax.nn.gelu(
            jnp.dot(normed, w_up_rows, preferred_element_type=jnp.float32), approximate=True
        ).astype(jnp.bfloat16)
        mlp_out = lax.psum(
            jnp.dot(act, w_down_cols, preferred_element_type=jnp.float32).astype(jnp.bfloat16), "mp"
        ).astype(jnp.float32)
        velocity = jnp.dot(
            (hidden_in + mlp_out).astype(jnp.bfloat16),
            w_out_full,
            preferred_element_type=jnp.float32,
        )
        latent_state = latent_state - step_size * velocity + noise_gain * step_noise[step_index]
    image_cols = 2 * tok_sample
    tile_cols = image_cols // mp_count
    images = (
        latent_state.reshape(samples_here, tok_sample, 2, 2, LAT_CH)
        .transpose(0, 2, 1, 3, 4)
        .reshape(samples_here, 2, image_cols, LAT_CH)
        * LATENT_SCALE
    )
    widened = jnp.pad(images, ((0, 0), (0, 0), (2, 2), (0, 0)))
    latent_tile = lax.dynamic_slice_in_dim(widened, mp_index * tile_cols, tile_cols + 4, 2)
    slot_count = 2 * samples_here
    first_slot = segment_index * slot_count
    slot_ids = first_slot + jnp.arange(slot_count, dtype=jnp.int32)
    slot_picks = (slot_map[None, :] == slot_ids[:, None]).astype(jnp.float32)
    flat_tile = latent_tile.reshape(samples_here, -1)
    owned = jnp.dot(
        slot_picks,
        lax.all_gather(flat_tile, "segment", axis=0, tiled=True),
        preferred_element_type=jnp.float32,
        precision=lax.Precision.HIGHEST,
    )
    decoded = decode_tile(
        owned.reshape(slot_count, 2, tile_cols + 4, LAT_CH),
        tile_cols,
        image_cols,
        conv_in_w,
        gn_gain,
        conv_mid_w,
    )
    return (latent_state, decoded)


ROWS = 48
MIB = 1 << 20


def xor_pieces(value, axis, masks):
    count = lax.axis_size(axis)
    moved = []
    for mask in masks:
        moved.append(lax.ppermute(value, axis, [(i, i ^ mask) for i in range(count)]))
    return moved


def split_three(value):
    high = value.astype(jnp.bfloat16)
    rest = value - high.astype(jnp.float32)
    middle = rest.astype(jnp.bfloat16)
    low = (rest - middle.astype(jnp.float32)).astype(jnp.bfloat16)
    return high, middle, low


def dot32(left, right):
    return jnp.dot(left, right, preferred_element_type=jnp.float32)


def dot_exact(value, exact):
    high, middle, low = split_three(value)
    return dot32(high, exact) + dot32(middle, exact) + dot32(low, exact)


def whole(shape_count):
    return [pl.BlockSpec(memory_space=pltpu.VMEM)] * shape_count


def split_kernel(cfg, *refs):
    segments, quarter = cfg
    w_in_ref, w_out_ref, prompt_ref, time_ref, ln_ref, w_up_ref, w_down_ref, pack_ref = refs[:8]
    outs = refs[8:]
    mine = lax.axis_index("segment")
    rows = w_up_ref.shape[0]
    half = rows // 2
    width = w_in_ref.shape[1]
    in_rows = w_in_ref.shape[0]
    prompt_rows = prompt_ref.shape[0]
    pack_ref[...] = jnp.zeros_like(pack_ref)
    pack_ref[0:in_rows] = w_in_ref[...]
    pack_ref[in_rows : 2 * in_rows] = w_out_ref[...]
    row = lax.broadcasted_iota(jnp.int32, (16, width), 0)
    others = jnp.where(
        row == prompt_rows,
        time_ref[...].astype(jnp.float32).reshape(1, width),
        jnp.where(row == prompt_rows + 1, ln_ref[...].astype(jnp.float32).reshape(1, width), 0.0),
    )
    for index in range(prompt_rows):
        others = jnp.where(
            row == index, prompt_ref[index : index + 1, :].astype(jnp.float32), others
        )
    pack_ref[2 * in_rows : 2 * in_rows + 16] = others.astype(jnp.bfloat16)
    above = rows + half
    for other in range(segments):
        out_ref = outs[other]
        target = lax.bitwise_xor(mine, other)
        start = pl.multiple_of(target * quarter, quarter)
        for index in range(w_down_ref.shape[1] // 128):
            out_ref[above + index * quarter : above + (index + 1) * quarter, :] = w_down_ref[
                pl.ds(start, quarter), index * 128 : (index + 1) * 128
            ]
        for part in range(segments):

            @pl.when(target == part)
            def _():
                block = w_up_ref[:, part * quarter : (part + 1) * quarter]
                out_ref[0:rows, :] = block[:, 0:128]
                tail = block[:, 128:quarter]
                out_ref[rows : rows + half, 0:64] = tail[0:half]
                out_ref[rows : rows + half, 64:128] = tail[half:rows]


def bring(copies):
    for copy in copies:
        copy.start()
    for copy in copies:
        copy.wait()


def table_kernel(cfg, *refs):
    segments, features, slices, latent, prompts = cfg
    own_ref, other_ref, scaled_ref, table_ref, w_out_ref, own, other, canon, sems = refs
    seg = lax.axis_index("segment")
    mp = lax.axis_index("mp")
    bring(
        [
            pltpu.make_async_copy(own_ref, own, sems.at[0]),
            pltpu.make_async_copy(other_ref, other, sems.at[1]),
        ]
    )
    width = own_ref.shape[3]
    stack = segments * ROWS
    in_rows = latent // segments
    prompt_rows = prompts // segments
    column = lax.broadcasted_iota(jnp.int32, (256, stack), 1)
    block = jnp.zeros_like(column)
    for edge in range(1, segments):
        block = block + (column >= edge * ROWS).astype(jnp.int32)
    inner = column - block * ROWS
    source = lax.bitwise_xor(block, seg)
    target = jnp.where(
        inner < in_rows,
        source * in_rows + inner,
        jnp.where(
            inner < 2 * in_rows,
            192 + source * in_rows + inner - in_rows,
            jnp.where(
                inner < 2 * in_rows + prompt_rows,
                64 + source * prompt_rows + inner - 2 * in_rows,
                jnp.where(
                    (block == 0) & (inner < 2 * in_rows + prompt_rows + 2),
                    64 + prompts + inner - 2 * in_rows - prompt_rows,
                    1000,
                ),
            ),
        ),
    )
    row = lax.broadcasted_iota(jnp.int32, (256, stack), 0)
    place = (row == target).astype(jnp.float32).astype(jnp.bfloat16)
    total = jnp.zeros((128, 1), jnp.float32)
    for index in range(slices):
        ref = own if index % 2 == 0 else other
        where_to = lax.bitwise_xor(mp, index)
        both = dot32(place, ref[index // 2].reshape(stack, width))
        canon[where_to] = both[0:128]
        table_ref[where_to] = both[0:80].astype(jnp.bfloat16)
        start = pl.multiple_of(where_to * width, width)
        w_out_ref[pl.ds(start, width), :] = jnp.transpose(both[128:256]).astype(jnp.bfloat16)
        total = total + jnp.sum(both[0:128], axis=1, keepdims=True)
    average = total / features
    for index in range(slices):
        part = canon[index]
        scaled = (part - average) * part[64 + prompts + 1 : 64 + prompts + 2, :]
        high = scaled.astype(jnp.bfloat16)
        scaled_ref[index, 0:128] = high
        scaled_ref[index, 128:256] = (scaled - high.astype(jnp.float32)).astype(jnp.bfloat16)


def combine_kernel(cfg, *refs):
    segments, slices, width, quarter = cfg
    scaled_ref, w_out_ref = refs[:2]
    sources = refs[2 : 2 + segments]
    piece_ref = refs[2 + segments]
    blocks, sems = refs[3 + segments :]
    seg = lax.axis_index("segment")
    bring(
        [pltpu.make_async_copy(sources[i], blocks.at[i], sems.at[i]) for i in range(segments)]
    )
    per_segment = slices // segments
    rows = per_segment * width
    above = rows + rows // 2
    main = jnp.zeros((128, 128), jnp.float32)
    tail = jnp.zeros((128, 128), jnp.float32)
    down = jnp.zeros((quarter, 128), jnp.float32)
    for other in range(segments):
        source_seg = lax.bitwise_xor(seg, other)
        for unit in range(per_segment):
            both = scaled_ref[source_seg * per_segment + unit]
            product = dot32(both, blocks[other, unit * width : (unit + 1) * width, :])
            main = main + product[0:128] + product[128:256]
            product = dot32(both, blocks[other, rows:above, :])
            product = product[0:128] + product[128:256]
            tail = tail + (product if unit == 0 else pltpu.roll(product, 64, 1))
        for index in range(rows // 128):
            start = pl.multiple_of(source_seg * rows + index * 128, 128)
            at = above + index * quarter
            down = down + dot32(
                blocks[other, at : at + quarter, :], w_out_ref[pl.ds(start, 128), :]
            )
    lane = lax.broadcasted_iota(jnp.int32, (1, 128), 1)
    down = 0.5 * down
    piece_ref[0:128, :] = jnp.where(lane < 64, jnp.transpose(main), down[0:128]).astype(
        jnp.bfloat16
    )
    piece_ref[128:192, :] = jnp.where(
        lane < 64, jnp.transpose(tail)[0:64], down[128:192]
    ).astype(jnp.bfloat16)
    piece_ref[192:208, :] = main[64:80].astype(jnp.bfloat16)
    piece_ref[208:224, :] = tail[64:80].astype(jnp.bfloat16)


def loop_kernel(cfg, *refs):
    features, slices, prompts, chunk = cfg
    assign_ref, noise_ref, step_ref, table_ref, w_out_ref = refs[:5]
    pieces = refs[5:-9]
    result_ref, state, steps, const, hidden, weights, extras, turned, sems = refs[-9:]
    mp = lax.axis_index("mp")
    tokens = state.shape[0]
    width = table_ref.shape[2]
    pair = lax.shift_right_logical(mp, 1)
    odd = lax.bitwise_and(mp, 1)
    copies = []
    for i, ref in enumerate(pieces):
        copies.append(
            pltpu.make_async_copy(ref.at[:, 0:192, :], weights.at[i], sems.at[2 * i])
        )
        copies.append(
            pltpu.make_async_copy(ref.at[:, 192:224, :], extras.at[i], sems.at[2 * i + 1])
        )
    for copy in copies:
        copy.start()
    prompt = assign_ref[mp]
    lane = lax.broadcasted_iota(jnp.int32, (1, 128), 1)
    lanes_from = pl.multiple_of(pair * 128, 128)
    rows_from = pl.multiple_of(odd * tokens, tokens)
    steps[...] = jnp.zeros_like(steps)
    state[...] = jnp.zeros_like(state)
    turned[...] = jnp.transpose(noise_ref[:, pl.ds(lanes_from, 128)])
    state[:, 0:64] = turned[pl.ds(rows_from, tokens), :]
    for index in range(STEPS):
        turned[...] = jnp.transpose(step_ref[index, :, pl.ds(lanes_from, 128)])
        steps[index, :, 0:64] = turned[pl.ds(rows_from, tokens), :]
    sixteen = lax.broadcasted_iota(jnp.int32, (16, 1), 0)
    pick = (sixteen == prompt).astype(jnp.float32)
    timing = (sixteen == prompts).astype(jnp.float32)
    for copy in copies:
        copy.wait()
    flat = [(i, j) for i in range(len(pieces)) for j in range(weights.shape[1])]
    for two in range(len(flat) // 2):
        e = [
            extras[flat[two * 2 + h][0], flat[two * 2 + h][1], 16 * i : 16 * i + 16, :].astype(
                jnp.float32
            )
            for h in range(2)
            for i in range(2)
        ]
        moved = pltpu.roll(e[2], 64, 1)
        lanes = [
            e[0],
            jnp.where(lane < 64, e[1], moved),
            jnp.where(lane < 64, moved, pltpu.roll(e[3], 64, 1)),
        ]
        for third in range(3):
            at = two * 384 + third * 128
            const[0:1, at : at + 128] = jnp.sum(pick * lanes[third], axis=0, keepdims=True)
            const[1:2, at : at + 128] = jnp.sum(timing * lanes[third], axis=0, keepdims=True)
    count = len(flat) * 192
    step_size = 1.0 / STEPS
    noise_gain = NOISE_SCALE * math.sqrt(step_size)

    def one_step(step, carry):
        time_now = 1.0 - step.astype(jnp.float32) * step_size
        now = state[...]
        operand = now.astype(jnp.bfloat16)
        narrow = operand[:, 0:64]
        weight = pick + time_now * timing
        total = jnp.zeros((tokens, 1), jnp.float32)
        for index in range(slices):
            base = jnp.sum(
                table_ref[index, 64:80, :].astype(jnp.float32) * weight, axis=0, keepdims=True
            )
            value = dot32(narrow, table_ref[index, 0:64, :]) + base
            hidden[index] = value
            total = total + jnp.sum(value, axis=1, keepdims=True)
        average = total / features
        square = jnp.zeros((tokens, 1), jnp.float32)
        velocity = jnp.zeros((tokens, 128), jnp.float32)
        for index in range(slices):
            value = hidden[index]
            centered = value - average
            square = square + jnp.sum(centered * centered, axis=1, keepdims=True)
            velocity = velocity + dot32(
                value.astype(jnp.bfloat16), w_out_ref[index * width : (index + 1) * width, :]
            )
        spread = lax.rsqrt(square / features + EPSILON)
        per_block = weights.shape[1] * 192
        for at in range(0, count, chunk):
            block = at // per_block
            inside = (at % per_block) // 192
            part = weights[block, inside : inside + chunk // 192].reshape(chunk, 128)
            shift = const[0:1, at : at + chunk] + time_now * const[1:2, at : at + chunk]
            pre = lax.dot_general(
                operand, part, (((1,), (1,)), ((), ())), preferred_element_type=jnp.float32
            )
            pre = (pre + shift) * spread
            inner = pre * (GELU_A + GELU_B * (pre * pre))
            act = (pre + pre * jnp.tanh(inner)).astype(jnp.bfloat16)
            velocity = velocity + dot32(act, part)
        moved = pltpu.roll(velocity, 64, 1)
        fresh = now - step_size * moved + noise_gain * steps[step]
        state[...] = jnp.where(lane < 64, fresh, 0.0)
        return carry

    lax.fori_loop(0, STEPS, one_step, 0)
    half = tokens // 2
    result_ref[...] = state[0:half] + pltpu.roll(state[half:tokens], 64, 1)


def patches_of(piece):
    lane = lax.broadcasted_iota(jnp.int32, (1, 128), 1)
    low = jnp.where(lane < 64, piece, 0.0)
    high = jnp.where(lane < 64, pltpu.roll(piece, 64, 1), 0.0)
    image = jnp.concatenate([low, high], axis=0) * LATENT_SCALE
    tokens = image.shape[0]
    row = lax.broadcasted_iota(jnp.int32, (tokens, 128), 0)
    before = jnp.where(row == 0, 0.0, pltpu.roll(image, 1, 0))
    after = jnp.where(row == tokens - 1, 0.0, pltpu.roll(image, tokens - 1, 0))
    odd = lax.bitwise_and(lax.shift_right_logical(lane, 4), 1) == 1
    beside = pltpu.roll(jnp.where(odd, before, after), 64, 1)
    return (image + beside).astype(jnp.bfloat16)


def decode_kernel(cfg, *refs):
    _, mp_count, samples_here, image_cols = cfg
    (map_ref, own_ref, other_ref, conv_in_ref, gain_ref, conv_mid_any, latents_ref, out_ref,
     table, received, patches, front, sums, squares, means, act, center, lines, conv_mid_ref,
     sems) = refs
    seg = lax.axis_index("segment")
    mp = lax.axis_index("mp")
    slots = out_ref.shape[0]
    half_pieces = own_ref.shape[0]
    pieces = 2 * half_pieces
    tokens = 2 * own_ref.shape[1]
    tile = out_ref.shape[2]
    tile_tokens = tile // 2
    lats = LAT_CH
    weight_copy = pltpu.make_async_copy(conv_mid_any, conv_mid_ref, sems.at[0])
    weight_copy.start()
    arrivals = [
        pltpu.make_async_copy(own_ref, received.at[0:half_pieces], sems.at[1]),
        pltpu.make_async_copy(other_ref, received.at[half_pieces:pieces], sems.at[2]),
    ]
    for copy in arrivals:
        copy.start()
    for slot in range(slots):
        table[slot] = pieces
    z_count = mp_count // 2
    for sample in range(map_ref.shape[0]):
        owner = lax.bitwise_xor(mp, sample % samples_here)
        place = (
            lax.bitwise_and(owner, 1) * half_pieces
            + lax.bitwise_xor(seg, sample // samples_here) * z_count
            + lax.shift_right_logical(owner, 1)
        )
        relative = map_ref[sample] - seg * slots

        @pl.when((relative >= 0) & (relative < slots))
        def _():
            table[relative] = place

    received[pieces] = jnp.zeros_like(received[0])
    front[...] = jnp.zeros_like(front)
    for group in range(8):
        if group < 4:
            row_in, offset = group // 2, group % 2
        else:
            row_in, offset = (group - 4) // 2, 2 if group % 2 == 0 else -1
        for out in range(4):
            row_out, col_out = out // 2, out % 2
            i, j = row_in - row_out + 1, offset - col_out + 1
            if 0 <= j <= 2:
                front[group * lats : (group + 1) * lats, out * VC : (out + 1) * VC] = (
                    conv_in_ref[i, j]
                )
    for copy in arrivals:
        copy.wait()
    for slot in range(slots):
        patch = patches_of(received[table[slot]])
        patches[slot] = patch
        sums[slot : slot + 1, :] = jnp.sum(patch.astype(jnp.float32), axis=0, keepdims=True)
    lane = lax.broadcasted_iota(jnp.int32, (1, 128), 1)
    half = tokens // 2
    for core in range(2):
        for line in range(z_count):
            piece = received[core * half_pieces + line]
            to = lax.bitwise_xor(lax.shift_right_logical(mp, 1), line)
            at = lax.bitwise_xor(lax.bitwise_and(mp, 1), core) * tokens
            lines[to, pl.ds(pl.multiple_of(at, tokens), half), :] = piece
            lines[to, pl.ds(pl.multiple_of(at + half, half), half), :] = pltpu.roll(piece, 64, 1)
    for line in range(z_count):
        block = jnp.transpose(lines[line])
        latents_ref[:, line * 128 : (line + 1) * 128] = block[0:64]
    per_group = VC // GROUPS
    entries = 2 * image_cols * per_group
    row_c = lax.broadcasted_iota(jnp.int32, (VC, VC), 0) // per_group
    col_c = lax.broadcasted_iota(jnp.int32, (VC, VC), 1) // per_group
    same = (row_c == col_c).astype(jnp.float32).astype(jnp.bfloat16)
    wide = dot_exact(sums[...], front[...])
    wide = wide[:, 0:VC] + wide[:, VC : 2 * VC] + wide[:, 2 * VC : 3 * VC] + wide[:, 3 * VC :]
    average = dot_exact(wide, same) / entries
    means[...] = average

    def one_slot(slot, carry):
        patch = patches[slot]
        mean = means[pl.ds(slot, 1), :]
        collected = None
        for out in range(4):
            value = dot32(patch, front[:, out * VC : (out + 1) * VC]) - mean
            value = value * value
            part = value[0:8]
            for at in range(8, tokens, 8):
                part = part + value[at : at + 8]
            collected = part if collected is None else collected + part
        squares[pl.ds(slot, 1), :] = jnp.sum(collected, axis=0, keepdims=True)
        return carry

    lax.fori_loop(0, slots, one_slot, 0)
    variance = dot_exact(squares[...], same) / entries
    spread = lax.rsqrt(variance + EPSILON)
    gain = gain_ref[...]
    count = (tile_tokens + 2) * slots
    row_t = lax.broadcasted_iota(jnp.int32, (count, 1), 0)
    token = row_t // slots
    slot_of = row_t - token * slots
    token = token + mp * tile_tokens - 1
    inside = (token >= 0) & (token < tokens)
    wanted = jnp.where(inside, slot_of * tokens + token, -1)
    column = lax.broadcasted_iota(jnp.int32, (count, slots * tokens), 1)
    pick = (column == wanted).astype(jnp.float32).astype(jnp.bfloat16)
    rows = dot32(pick, patches[...].reshape(slots * tokens, 128)).astype(jnp.bfloat16)
    for out in range(4):
        row_out, col_out = out // 2, out % 2
        value = dot32(rows, front[:, out * VC : (out + 1) * VC])
        for t in range(tile_tokens + 2):
            part = value[t * slots : (t + 1) * slots]
            at = (2 * t + col_out) * slots
            if 1 <= t <= tile_tokens:
                center[row_out, at - 2 * slots : at - slots, :] = part
            scaled = (part - average) * spread * gain
            silu = 0.5 * scaled * (1.0 + jnp.tanh(0.5 * scaled))
            if t == 0:
                silu = jnp.where(mp == 0, 0.0, silu)
            if t == tile_tokens + 1:
                silu = jnp.where(mp == mp_count - 1, 0.0, silu)
            act[row_out, at : at + slots, :] = silu.astype(jnp.bfloat16)
    weight_copy.wait()
    size = tile * slots
    row_p = lax.broadcasted_iota(jnp.int32, (size, size), 0)
    col_p = lax.broadcasted_iota(jnp.int32, (size, size), 1)
    slot_p = row_p // tile
    swap = (col_p == (row_p - slot_p * tile) * slots + slot_p).astype(jnp.float32)
    swap = swap.astype(jnp.bfloat16)
    for row_out in range(2):
        total = center[row_out]
        for row_in in range(2):
            for shift in range(3):
                at = (1 + shift) * slots
                total = total + dot32(
                    act[row_in, at : at + size, :], conv_mid_ref[row_in - row_out + 1, shift]
                )
        ordered = dot32(swap, total.astype(jnp.bfloat16)).astype(jnp.bfloat16)
        out_ref[:, row_out, :, :] = ordered.reshape(slots, tile, VC)


def per_device_fast(
    noise_init,
    step_noise,
    assign,
    slot_map,
    prompt_embed,
    time_vec,
    w_in,
    ln_gain,
    w_up,
    w_down,
    w_out,
    conv_in_w,
    gn_gain,
    conv_mid_w,
):
    segments = lax.axis_size("segment")
    mp_count = lax.axis_size("mp")
    around = range(1, segments)
    along = range(2, mp_count, 2)
    width = w_in.shape[1]
    features = width * mp_count
    latent = w_in.shape[0] * segments
    prompts = prompt_embed.shape[0] * segments
    samples_here = assign.shape[0]
    tok_group = noise_init.shape[0]
    tokens = tok_group // mp_count
    hidden = w_up.shape[1]
    quarter = hidden // segments
    bf16, f32 = jnp.bfloat16, jnp.float32
    any_space = pl.BlockSpec(memory_space=pl.ANY)
    smem = pl.BlockSpec(memory_space=pltpu.SMEM)
    joint = w_up.shape[0] * 3 // 2 + quarter * (w_down.shape[1] // 128)
    pack, *split = pl.pallas_call(
        functools.partial(split_kernel, (segments, quarter)),
        out_shape=[jax.ShapeDtypeStruct((ROWS, width), bf16)]
        + [jax.ShapeDtypeStruct((joint, 128), bf16)] * segments,
        in_specs=whole(7),
        out_specs=whole(1 + segments),
        name="split_weights",
    )(w_in, w_out.T, prompt_embed, time_vec, ln_gain, w_up, w_down)
    table = jnp.stack([pack] + xor_pieces(pack, "segment", around))
    sources = [split[0]]
    for other in around:
        sources += xor_pieces(split[other], "segment", [other])
    table = jnp.stack([table] + xor_pieces(table, "mp", along))
    (table_other,) = xor_pieces(table, "mp", [1])
    scaled, tables, w_out_all = pl.pallas_call(
        functools.partial(table_kernel, (segments, features, mp_count, latent, prompts)),
        out_shape=[
            jax.ShapeDtypeStruct((mp_count, 256, width), bf16),
            jax.ShapeDtypeStruct((mp_count, 80, width), bf16),
            jax.ShapeDtypeStruct((features, 128), bf16),
        ],
        in_specs=[any_space] * 2,
        out_specs=whole(3),
        scratch_shapes=[
            pltpu.VMEM(table.shape, bf16),
            pltpu.VMEM(table.shape, bf16),
            pltpu.VMEM((mp_count, 128, width), f32),
            pltpu.SemaphoreType.DMA((2,)),
        ],
        compiler_params=pltpu.CompilerParams(vmem_limit_bytes=16 * MIB),
        name="order_tables",
    )(table, table_other)
    piece = pl.pallas_call(
        functools.partial(combine_kernel, (segments, mp_count, width, quarter)),
        out_shape=jax.ShapeDtypeStruct((quarter + 32, 128), bf16),
        in_specs=whole(2) + [any_space] * segments,
        out_specs=whole(1)[0],
        scratch_shapes=[
            pltpu.VMEM((segments, joint, 128), bf16),
            pltpu.SemaphoreType.DMA((segments,)),
        ],
        compiler_params=pltpu.CompilerParams(vmem_limit_bytes=16 * MIB),
        name="combine_weights",
    )(scaled, w_out_all, *sources)
    line = jnp.stack([piece] + xor_pieces(piece, "mp", along))
    plane = [line]
    for other in around:
        plane += xor_pieces(line, "segment", [other])
    plane = plane + [xor_pieces(block, "mp", [1])[0] for block in plane]
    half = mp_count // 2
    result = pl.pallas_call(
        functools.partial(loop_kernel, (features, mp_count, prompts, 384)),
        out_shape=jax.ShapeDtypeStruct((tokens // 2, 128), f32),
        in_specs=[smem] + whole(4) + [any_space] * len(plane),
        out_specs=whole(1)[0],
        scratch_shapes=[
            pltpu.VMEM((tokens, 128), f32),
            pltpu.VMEM((STEPS, tokens, 128), f32),
            pltpu.VMEM((8, len(plane) * half * quarter), f32),
            pltpu.VMEM((mp_count, tokens, width), f32),
            pltpu.VMEM((len(plane), half, quarter, 128), bf16),
            pltpu.VMEM((len(plane), half, 32, 128), bf16),
            pltpu.VMEM((128, 64), f32),
            pltpu.SemaphoreType.DMA((2 * len(plane),)),
        ],
        compiler_params=pltpu.CompilerParams(vmem_limit_bytes=24 * MIB),
        name="denoise",
    )(assign, noise_init.T, step_noise.transpose(0, 2, 1), tables, w_out_all, *plane)
    image = jnp.stack([result] + xor_pieces(result, "mp", along))
    image = jnp.concatenate([image] + xor_pieces(image, "segment", around), axis=0)
    (image_other,) = xor_pieces(image, "mp", [1])
    image_cols = 2 * tokens
    tile = image_cols // mp_count
    slots = 2 * samples_here
    pieces = segments * mp_count
    latents, decoded = pl.pallas_call(
        functools.partial(decode_kernel, (segments, mp_count, samples_here, image_cols)),
        out_shape=[
            jax.ShapeDtypeStruct((64, tok_group), f32),
            jax.ShapeDtypeStruct((slots, 2, tile, VC), bf16),
        ],
        in_specs=[smem, any_space, any_space] + whole(2) + [any_space],
        out_specs=whole(2),
        scratch_shapes=[
            pltpu.SMEM((slots,), jnp.int32),
            pltpu.VMEM((pieces + 1, tokens // 2, 128), f32),
            pltpu.VMEM((slots, tokens, 128), bf16),
            pltpu.VMEM((128, 4 * VC), bf16),
            pltpu.VMEM((slots, 128), f32),
            pltpu.VMEM((slots, VC), f32),
            pltpu.VMEM((slots, VC), f32),
            pltpu.VMEM((2, (tile + 4) * slots, VC), bf16),
            pltpu.VMEM((2, tile * slots, VC), f32),
            pltpu.VMEM((half, 128, 128), f32),
            pltpu.VMEM(conv_mid_w.shape, bf16),
            pltpu.SemaphoreType.DMA((3,)),
        ],
        compiler_params=pltpu.CompilerParams(vmem_limit_bytes=40 * MIB),
        name="decode",
    )(slot_map, image, image_other, conv_in_w, gn_gain[None, :], conv_mid_w)
    return latents.T, decoded


def choose(*args):
    segments, mp_count = lax.axis_size("segment"), lax.axis_size("mp")
    noise, assign, prompt, w_in, w_up = (args[i].shape for i in (0, 2, 4, 6, 8))
    ready = (
        mp_count == 2 * segments == 8
        and noise[0] // mp_count == noise[0] // assign[0] == 64
        and w_up[1] // segments == w_in[1] == 192
        and w_in[0] * segments == noise[1] == 64
        and prompt[0] * segments <= 8
    )
    return (per_device_fast if ready else per_device)(*args)


def solution(mesh):
    return jax.shard_map(
        choose,
        mesh=mesh,
        in_specs=(
            P("segment", None),
            P(None, "segment", None),
            P("segment"),
            P(),
            P("segment", "mp"),
            P("mp"),
            P("segment", "mp"),
            P("mp"),
            P("segment", "mp"),
            P("mp", "segment"),
            P("mp", "segment"),
            P(),
            P(),
            P(),
        ),
        out_specs=(P("segment", None), P("segment", None, "mp", None)),
        check_vma=False,
    )
```

```python
import functools
import math

import jax
import jax.numpy as jnp
from jax import lax
from jax.experimental import pallas as pl
from jax.experimental.pallas import tpu as pltpu
from jax.sharding import PartitionSpec as P

LAT_CH = 16
VC = 512
GROUPS = 32
STEPS = 4


NOISE_SCALE = 0.5
LATENT_SCALE = 1.0 / 1.5305
EPSILON = 1e-06
GELU_A = math.sqrt(2.0 / math.pi)
GELU_S = (GELU_A * 0.044715) ** (1.0 / 3.0)
GELU_C = GELU_A / GELU_S


def with_halo(cells, sides, width):
    for axis, dim in sides:
        count = lax.axis_size(axis)
        ends = count - 1
        head = lax.slice_in_dim(cells, 0, width, axis=dim)
        tail = lax.slice_in_dim(cells, cells.shape[dim] - width, cells.shape[dim], axis=dim)
        cells = jnp.concatenate(
            [
                lax.ppermute(tail, axis, [(i, (i + 1) % count) for i in range(ends)]),
                cells,
                lax.ppermute(head, axis, [((i + 1) % count, i) for i in range(ends)]),
            ],
            axis=dim,
        )
    return cells


def conv_rows(padded, weight, col_count):
    accumulated = None
    for row_shift in range(3):
        for col_shift in range(3):
            window = padded[:, row_shift : row_shift + 2, col_shift : col_shift + col_count, :]
            product = jnp.einsum(
                "nrcv,vw->nrcw",
                window,
                weight[row_shift, col_shift],
                preferred_element_type=jnp.float32,
            )
            accumulated = product if accumulated is None else accumulated + product
    return accumulated


def decode_tile(latent_tile, tile_cols, image_cols, conv_in_w, gn_gain, conv_mid_w):
    slot_rows = latent_tile.shape[0]
    padded = jnp.pad(latent_tile.astype(jnp.bfloat16), ((0, 0), (1, 1), (0, 0), (0, 0)))
    first_wide = conv_rows(padded, conv_in_w, tile_cols + 2)
    conv_first = first_wide[:, :, 1 : tile_cols + 1, :]
    per_group = VC // GROUPS
    grouped = conv_first.reshape(slot_rows, 2 * tile_cols, GROUPS, per_group)
    group_sum, group_square = lax.psum(
        (jnp.sum(grouped, axis=(1, 3)), jnp.sum(grouped * grouped, axis=(1, 3))), "mp"
    )
    entries = 2 * image_cols * per_group
    average = group_sum / entries
    variance = jnp.maximum(group_square / entries - average * average, 0.0)
    inv_spread = lax.rsqrt(variance + EPSILON)
    col_count = conv_first.shape[2]
    shaped = conv_first.reshape(slot_rows, 2, col_count, GROUPS, per_group)
    shaped = (shaped - average[:, None, None, :, None]) * inv_spread[:, None, None, :, None]
    activated = jax.nn.silu(shaped.reshape(slot_rows, 2, col_count, VC) * gn_gain).astype(
        jnp.bfloat16
    )
    act_wide = with_halo(activated, (("mp", 2),), 1)
    act_padded = jnp.pad(act_wide, ((0, 0), (1, 1), (0, 0), (0, 0)))
    return (conv_first + conv_rows(act_padded, conv_mid_w, tile_cols)).astype(jnp.bfloat16)


def full_front(
    latent_state,
    w_in_full,
    prompt_cond,
    time_full,
    gain_full,
    time_now,
    samples_here,
    tok_sample,
    tok_group,
):
    embedded = jnp.dot(
        latent_state.astype(jnp.bfloat16), w_in_full, preferred_element_type=jnp.float32
    )
    hidden_in = (embedded.reshape(samples_here, tok_sample, -1) + prompt_cond[:, None, :]).reshape(
        tok_group, -1
    ) + time_now * time_full.astype(jnp.float32)
    average = jnp.mean(hidden_in, axis=-1, keepdims=True)
    centered = hidden_in - average
    variance = jnp.mean(centered * centered, axis=-1, keepdims=True)
    normed = (centered * lax.rsqrt(variance + EPSILON) * gain_full.astype(jnp.float32)).astype(
        jnp.bfloat16
    )
    return (hidden_in, normed)


def per_device(
    noise_init,
    step_noise,
    assign,
    slot_map,
    prompt_embed,
    time_vec,
    w_in,
    ln_gain,
    w_up,
    w_down,
    w_out,
    conv_in_w,
    gn_gain,
    conv_mid_w,
):
    mp_count = lax.axis_size("mp")
    mp_index = lax.axis_index("mp")
    segment_index = lax.axis_index("segment")
    w_in_rows, w_up_rows, w_down_cols, w_out_cols, prompt_rows = (
        lax.all_gather(w_in, "segment", axis=0, tiled=True),
        lax.all_gather(w_up, "segment", axis=0, tiled=True),
        lax.all_gather(w_down, "segment", axis=1, tiled=True),
        lax.all_gather(w_out, "segment", axis=1, tiled=True),
        lax.all_gather(prompt_embed, "segment", axis=0, tiled=True),
    )
    samples_here = assign.shape[0]
    tok_group = noise_init.shape[0]
    tok_sample = tok_group // samples_here
    prompt_count = prompt_rows.shape[0]
    choose = (assign[:, None] == jnp.arange(prompt_count, dtype=jnp.int32)[None, :]).astype(
        jnp.bfloat16
    )
    step_size = 1.0 / STEPS
    noise_gain = NOISE_SCALE * math.sqrt(step_size)
    latent_state = noise_init
    w_in_full, prompt_full, w_out_full, time_full, gain_full = (
        lax.all_gather(w_in_rows, "mp", axis=1, tiled=True),
        lax.all_gather(prompt_rows, "mp", axis=1, tiled=True),
        lax.all_gather(w_out_cols, "mp", axis=0, tiled=True),
        lax.all_gather(time_vec, "mp", axis=0, tiled=True),
        lax.all_gather(ln_gain, "mp", axis=0, tiled=True),
    )
    prompt_cond = jnp.dot(choose, prompt_full, preferred_element_type=jnp.float32)
    for step_index in range(STEPS):
        time_now = 1.0 - step_index * step_size
        hidden_in, normed = full_front(
            latent_state,
            w_in_full,
            prompt_cond,
            time_full,
            gain_full,
            time_now,
            samples_here,
            tok_sample,
            tok_group,
        )
        act = jax.nn.gelu(
            jnp.dot(normed, w_up_rows, preferred_element_type=jnp.float32), approximate=True
        ).astype(jnp.bfloat16)
        mlp_out = lax.psum(
            jnp.dot(act, w_down_cols, preferred_element_type=jnp.float32).astype(jnp.bfloat16), "mp"
        ).astype(jnp.float32)
        velocity = jnp.dot(
            (hidden_in + mlp_out).astype(jnp.bfloat16),
            w_out_full,
            preferred_element_type=jnp.float32,
        )
        latent_state = latent_state - step_size * velocity + noise_gain * step_noise[step_index]
    image_cols = 2 * tok_sample
    tile_cols = image_cols // mp_count
    images = (
        latent_state.reshape(samples_here, tok_sample, 2, 2, LAT_CH)
        .transpose(0, 2, 1, 3, 4)
        .reshape(samples_here, 2, image_cols, LAT_CH)
        * LATENT_SCALE
    )
    widened = jnp.pad(images, ((0, 0), (0, 0), (2, 2), (0, 0)))
    latent_tile = lax.dynamic_slice_in_dim(widened, mp_index * tile_cols, tile_cols + 4, 2)
    slot_count = 2 * samples_here
    first_slot = segment_index * slot_count
    slot_ids = first_slot + jnp.arange(slot_count, dtype=jnp.int32)
    slot_picks = (slot_map[None, :] == slot_ids[:, None]).astype(jnp.float32)
    flat_tile = latent_tile.reshape(samples_here, -1)
    owned = jnp.dot(
        slot_picks,
        lax.all_gather(flat_tile, "segment", axis=0, tiled=True),
        preferred_element_type=jnp.float32,
        precision=lax.Precision.HIGHEST,
    )
    decoded = decode_tile(
        owned.reshape(slot_count, 2, tile_cols + 4, LAT_CH),
        tile_cols,
        image_cols,
        conv_in_w,
        gn_gain,
        conv_mid_w,
    )
    return (latent_state, decoded)


ROWS = 48
MIB = 1 << 20


def xor_pieces(value, axis, masks):
    count = lax.axis_size(axis)
    moved = []
    for mask in masks:
        moved.append(lax.ppermute(value, axis, [(i, i ^ mask) for i in range(count)]))
    return moved


def split_three(value):
    high = value.astype(jnp.bfloat16)
    rest = value - high.astype(jnp.float32)
    middle = rest.astype(jnp.bfloat16)
    low = (rest - middle.astype(jnp.float32)).astype(jnp.bfloat16)
    return high, middle, low


def dot32(left, right):
    return jnp.dot(left, right, preferred_element_type=jnp.float32)


def dot_exact(value, exact):
    high, middle, low = split_three(value)
    return dot32(high, exact) + dot32(middle, exact) + dot32(low, exact)


def whole(shape_count):
    return [pl.BlockSpec(memory_space=pltpu.VMEM)] * shape_count


def split_kernel(cfg, *refs):
    segments, quarter = cfg
    w_in_ref, w_out_ref, prompt_ref, time_ref, ln_ref, w_up_ref, w_down_ref, pack_ref = refs[:8]
    outs = refs[8:]
    mine = lax.axis_index("segment")
    rows = w_up_ref.shape[0]
    half = rows // 2
    width = w_in_ref.shape[1]
    in_rows = w_in_ref.shape[0]
    prompt_rows = prompt_ref.shape[0]
    pack_ref[...] = jnp.zeros_like(pack_ref)
    pack_ref[0:in_rows] = w_in_ref[...]
    pack_ref[in_rows : 2 * in_rows] = w_out_ref[...]
    row = lax.broadcasted_iota(jnp.int32, (16, width), 0)
    others = jnp.where(
        row == prompt_rows,
        time_ref[...].astype(jnp.float32).reshape(1, width),
        jnp.where(row == prompt_rows + 1, ln_ref[...].astype(jnp.float32).reshape(1, width), 0.0),
    )
    for index in range(prompt_rows):
        others = jnp.where(
            row == index, prompt_ref[index : index + 1, :].astype(jnp.float32), others
        )
    pack_ref[2 * in_rows : 2 * in_rows + 16] = others.astype(jnp.bfloat16)
    above = rows + half
    for other in range(segments):
        out_ref = outs[other]
        target = lax.bitwise_xor(mine, other)
        start = pl.multiple_of(target * quarter, quarter)
        for index in range(w_down_ref.shape[1] // 128):
            out_ref[above + index * quarter : above + (index + 1) * quarter, :] = w_down_ref[
                pl.ds(start, quarter), index * 128 : (index + 1) * 128
            ]
        for part in range(segments):

            @pl.when(target == part)
            def _():
                block = w_up_ref[:, part * quarter : (part + 1) * quarter]
                out_ref[0:rows, :] = block[:, 0:128]
                tail = block[:, 128:quarter]
                out_ref[rows : rows + half, 0:64] = tail[0:half]
                out_ref[rows : rows + half, 64:128] = tail[half:rows]


def bring(copies):
    for copy in copies:
        copy.start()
    for copy in copies:
        copy.wait()


def table_kernel(cfg, *refs):
    segments, features, slices, latent, prompts = cfg
    own_ref, other_ref, scaled_ref, table_ref, w_out_ref, own, other, canon, sems = refs
    seg = lax.axis_index("segment")
    mp = lax.axis_index("mp")
    bring(
        [
            pltpu.make_async_copy(own_ref, own, sems.at[0]),
            pltpu.make_async_copy(other_ref, other, sems.at[1]),
        ]
    )
    width = own_ref.shape[3]
    stack = segments * ROWS
    in_rows = latent // segments
    prompt_rows = prompts // segments
    column = lax.broadcasted_iota(jnp.int32, (256, stack), 1)
    block = jnp.zeros_like(column)
    for edge in range(1, segments):
        block = block + (column >= edge * ROWS).astype(jnp.int32)
    inner = column - block * ROWS
    source = lax.bitwise_xor(block, seg)
    target = jnp.where(
        inner < in_rows,
        source * in_rows + inner,
        jnp.where(
            inner < 2 * in_rows,
            128 + source * in_rows + inner - in_rows,
            jnp.where(
                inner < 2 * in_rows + prompt_rows,
                64 + source * prompt_rows + inner - 2 * in_rows,
                jnp.where(
                    (block == 0) & (inner < 2 * in_rows + prompt_rows + 2),
                    64 + prompts + inner - 2 * in_rows - prompt_rows,
                    -1,
                ),
            ),
        ),
    )
    row = lax.broadcasted_iota(jnp.int32, (256, stack), 0)
    again = (target >= 128) & (row == target + 64)
    place = ((row == target) | again).astype(jnp.float32).astype(jnp.bfloat16)
    total = jnp.zeros((128, 1), jnp.float32)
    for index in range(slices):
        ref = own if index % 2 == 0 else other
        where_to = lax.bitwise_xor(mp, index)
        both = dot32(place, ref[index // 2].reshape(stack, width))
        canon[where_to] = both[0:128]
        table_ref[where_to] = both[0:128].astype(jnp.bfloat16)
        start = pl.multiple_of(where_to * width, width)
        w_out_ref[pl.ds(start, width), :] = jnp.transpose(both[128:256]).astype(jnp.bfloat16)
        total = total + jnp.sum(both[0:128], axis=1, keepdims=True)
    average = total / features
    for index in range(slices):
        part = canon[index]
        scaled = (part - average) * part[64 + prompts + 1 : 64 + prompts + 2, :]
        high = scaled.astype(jnp.bfloat16)
        scaled_ref[index, 0:128] = high
        scaled_ref[index, 128:256] = (scaled - high.astype(jnp.float32)).astype(jnp.bfloat16)


def combine_kernel(cfg, *refs):
    segments, slices, width, quarter = cfg
    scaled_ref, w_out_ref = refs[:2]
    sources = refs[2 : 2 + segments]
    piece_ref = refs[2 + segments]
    blocks, sems = refs[3 + segments :]
    seg = lax.axis_index("segment")
    bring(
        [pltpu.make_async_copy(sources[i], blocks.at[i], sems.at[i]) for i in range(segments)]
    )
    per_segment = slices // segments
    rows = per_segment * width
    above = rows + rows // 2
    main = jnp.zeros((128, 128), jnp.float32)
    tail = jnp.zeros((128, 128), jnp.float32)
    down = jnp.zeros((quarter, 128), jnp.float32)
    for other in range(segments):
        source_seg = lax.bitwise_xor(seg, other)
        for unit in range(per_segment):
            both = scaled_ref[source_seg * per_segment + unit]
            product = dot32(both, blocks[other, unit * width : (unit + 1) * width, :])
            main = main + product[0:128] + product[128:256]
            product = dot32(both, blocks[other, rows:above, :])
            product = product[0:128] + product[128:256]
            tail = tail + (product if unit == 0 else pltpu.roll(product, 64, 1))
        for index in range(rows // 128):
            start = pl.multiple_of(source_seg * rows + index * 128, 128)
            at = above + index * quarter
            down = down + dot32(
                blocks[other, at : at + quarter, :], w_out_ref[pl.ds(start, 128), :]
            )
    lane = lax.broadcasted_iota(jnp.int32, (1, 128), 1)
    down = (0.5 / GELU_S) * down
    piece_ref[0:80, :] = main[0:80].astype(jnp.bfloat16)
    beside = pltpu.roll(tail, 64, 1)
    piece_ref[80:128, :] = jnp.where(lane < 64, tail[0:48], beside[32:80]).astype(jnp.bfloat16)
    piece_ref[128:192, :] = jnp.where(lane < 64, down[0:64], down[64:128]).astype(jnp.bfloat16)
    piece_ref[192:224, :] = jnp.where(lane < 64, down[128:160], down[160:192]).astype(
        jnp.bfloat16
    )


def moment_kernel(features, table_ref, w_out_ref, moment_ref):
    slices, rows, width = table_ref.shape
    total = jnp.zeros((rows, 1), jnp.float32)
    for index in range(slices):
        total = total + jnp.sum(table_ref[index].astype(jnp.float32), axis=1, keepdims=True)
    average = total / features
    gram = jnp.zeros((rows, rows), jnp.float32)
    velocity = jnp.zeros((rows, 128), jnp.float32)
    for index in range(slices):
        raw = table_ref[index]
        centered = raw.astype(jnp.float32) - average
        gram = gram + lax.dot_general(
            centered,
            centered,
            (((1,), (1,)), ((), ())),
            precision=lax.Precision.HIGHEST,
            preferred_element_type=jnp.float32,
        )
        velocity = velocity + dot32(raw, w_out_ref[index * width : (index + 1) * width, :])
    for index, part in enumerate(split_three(gram) + split_three(velocity)[:2]):
        moment_ref[:, index * 128 : (index + 1) * 128] = part


def loop_kernel(cfg, *refs):
    features, prompts = cfg
    assign_ref, noise_ref, step_ref, moment_ref = refs[:4]
    pieces = refs[4:-9]
    result_ref, state, steps, first, second, narrow, packed, turned, sems = refs[-9:]
    mp = lax.axis_index("mp")
    tokens = state.shape[0]
    pair = lax.shift_right_logical(mp, 1)
    odd = lax.bitwise_and(mp, 1)
    lines = narrow.shape[1]
    copies = []
    for i, ref in enumerate(pieces):
        for j in range(lines):
            at = i * 768 + (384 * (j % 2) + 128 * (j // 2))
            copies.append(
                pltpu.make_async_copy(
                    ref.at[j, 0:80, :], first.at[:, at : at + 128], sems.at[i, j]
                )
            )
        copies.append(
            pltpu.make_async_copy(ref.at[:, 80:128, :], narrow.at[i], sems.at[i, lines])
        )
        copies.append(
            pltpu.make_async_copy(ref.at[:, 128:224, :], packed.at[i], sems.at[i, lines + 1])
        )
    for copy in copies:
        copy.start()
    prompt = assign_ref[mp]
    lane = lax.broadcasted_iota(jnp.int32, (1, 128), 1)
    low = lane < 64
    lanes_from = pl.multiple_of(pair * 128, 128)
    rows_from = pl.multiple_of(odd * tokens, tokens)
    steps[...] = jnp.zeros_like(steps)
    state[...] = jnp.zeros_like(state)
    turned[...] = jnp.transpose(noise_ref[:, pl.ds(lanes_from, 128)])
    state[:, 0:64] = turned[pl.ds(rows_from, tokens), :]
    for index in range(STEPS):
        turned[...] = jnp.transpose(step_ref[index, :, pl.ds(lanes_from, 128)])
        steps[index, :, 0:64] = turned[pl.ds(rows_from, tokens), :]
    pick = (lane == 64 + prompt).astype(jnp.float32)
    timing = (lane == 64 + prompts).astype(jnp.float32)
    for copy in copies:
        copy.wait()

    def swap(value):
        return pltpu.roll(value.astype(jnp.float32), 64, 1).astype(jnp.bfloat16)

    for i in range(len(pieces)):
        for two in range(lines // 2):
            left, right = narrow[i, 2 * two], narrow[i, 2 * two + 1]
            at = i * 768 + 384 * two + 256
            first[0:48, at : at + 128] = jnp.where(low, left, swap(right))
            first[48:80, at : at + 128] = jnp.where(low, swap(left)[16:48], right[16:48])
            left, right = packed[i, 2 * two], packed[i, 2 * two + 1]
            at = i * 384 + 128 * two
            second[at : at + 64, :] = jnp.where(low, left[0:64], swap(right[0:64]))
            second[at + 64 : at + 128, :] = jnp.where(low, swap(left[0:64]), right[0:64])
            left, right = packed[i, two, 64:96], packed[i, two + 2, 64:96]
            at = i * 384 + 256 + 64 * two
            second[at : at + 32, :] = jnp.where(low, left, swap(right))
            second[at + 32 : at + 64, :] = jnp.where(low, swap(left), right)
    step_size = 1.0 / STEPS
    noise_gain = NOISE_SCALE * math.sqrt(step_size)

    def one_step(step, carry):
        time_now = 1.0 - step.astype(jnp.float32) * step_size
        now = state[...]
        full = (now + pick + time_now * timing).astype(jnp.bfloat16)
        moments = dot32(full, moment_ref[...])
        quadratic = moments[:, 0:128] + moments[:, 128:256] + moments[:, 256:384]
        square = jnp.sum(full.astype(jnp.float32) * quadratic, axis=1, keepdims=True)
        scale = GELU_S * lax.rsqrt(jnp.maximum(square / features, 0.0) + EPSILON)
        total = jnp.zeros((2 * tokens, 128), jnp.float32)
        for i in range(len(pieces)):
            acts = []
            for at in (i * 768, i * 768 + 384):
                pre = dot32(full[:, 0:80], first[:, at : at + 384]) * scale
                inner = pre * (GELU_C + pre * pre)
                acts.append((pre + pre * jnp.tanh(inner)).astype(jnp.bfloat16))
            total = total + dot32(
                jnp.concatenate(acts, axis=0), second[i * 384 : (i + 1) * 384, :]
            )
        velocity = moments[:, 384:512] + moments[:, 512:640]
        velocity = velocity + total[0:tokens] + pltpu.roll(total[tokens : 2 * tokens], 64, 1)
        fresh = now - step_size * velocity + noise_gain * steps[step]
        state[...] = jnp.where(low, fresh, 0.0)
        return carry

    lax.fori_loop(0, STEPS, one_step, 0)
    half = tokens // 2
    result_ref[...] = state[0:half] + pltpu.roll(state[half:tokens], 64, 1)


def patches_of(piece):
    lane = lax.broadcasted_iota(jnp.int32, (1, 128), 1)
    low = jnp.where(lane < 64, piece, 0.0)
    high = jnp.where(lane < 64, pltpu.roll(piece, 64, 1), 0.0)
    image = jnp.concatenate([low, high], axis=0) * LATENT_SCALE
    tokens = image.shape[0]
    row = lax.broadcasted_iota(jnp.int32, (tokens, 128), 0)
    before = jnp.where(row == 0, 0.0, pltpu.roll(image, 1, 0))
    after = jnp.where(row == tokens - 1, 0.0, pltpu.roll(image, tokens - 1, 0))
    odd = lax.bitwise_and(lax.shift_right_logical(lane, 4), 1) == 1
    beside = pltpu.roll(jnp.where(odd, before, after), 64, 1)
    return (image + beside).astype(jnp.bfloat16)


def decode_kernel(cfg, *refs):
    _, mp_count, samples_here, image_cols = cfg
    (map_ref, own_ref, other_ref, conv_in_ref, gain_ref, conv_mid_any, latents_ref, out_ref,
     table, received, patches, front, sums, squares, means, act, center, lines, conv_mid_ref,
     sems) = refs
    seg = lax.axis_index("segment")
    mp = lax.axis_index("mp")
    slots = out_ref.shape[0]
    half_pieces = own_ref.shape[0]
    pieces = 2 * half_pieces
    tokens = 2 * own_ref.shape[1]
    tile = out_ref.shape[2]
    tile_tokens = tile // 2
    lats = LAT_CH
    weight_copy = pltpu.make_async_copy(conv_mid_any, conv_mid_ref, sems.at[0])
    weight_copy.start()
    arrivals = [
        pltpu.make_async_copy(own_ref, received.at[0:half_pieces], sems.at[1]),
        pltpu.make_async_copy(other_ref, received.at[half_pieces:pieces], sems.at[2]),
    ]
    for copy in arrivals:
        copy.start()
    for slot in range(slots):
        table[slot] = pieces
    z_count = mp_count // 2
    for sample in range(map_ref.shape[0]):
        owner = lax.bitwise_xor(mp, sample % samples_here)
        place = (
            lax.bitwise_and(owner, 1) * half_pieces
            + lax.bitwise_xor(seg, sample // samples_here) * z_count
            + lax.shift_right_logical(owner, 1)
        )
        relative = map_ref[sample] - seg * slots

        @pl.when((relative >= 0) & (relative < slots))
        def _():
            table[relative] = place

    received[pieces] = jnp.zeros_like(received[0])
    front[...] = jnp.zeros_like(front)
    for group in range(8):
        if group < 4:
            row_in, offset = group // 2, group % 2
        else:
            row_in, offset = (group - 4) // 2, 2 if group % 2 == 0 else -1
        for out in range(4):
            row_out, col_out = out // 2, out % 2
            i, j = row_in - row_out + 1, offset - col_out + 1
            if 0 <= j <= 2:
                front[group * lats : (group + 1) * lats, out * VC : (out + 1) * VC] = (
                    conv_in_ref[i, j]
                )
    for copy in arrivals:
        copy.wait()
    for slot in range(slots):
        patch = patches_of(received[table[slot]])
        patches[slot] = patch
        sums[slot : slot + 1, :] = jnp.sum(patch.astype(jnp.float32), axis=0, keepdims=True)
    lane = lax.broadcasted_iota(jnp.int32, (1, 128), 1)
    half = tokens // 2
    for core in range(2):
        for line in range(z_count):
            piece = received[core * half_pieces + line]
            to = lax.bitwise_xor(lax.shift_right_logical(mp, 1), line)
            at = lax.bitwise_xor(lax.bitwise_and(mp, 1), core) * tokens
            lines[to, pl.ds(pl.multiple_of(at, tokens), half), :] = piece
            lines[to, pl.ds(pl.multiple_of(at + half, half), half), :] = pltpu.roll(piece, 64, 1)
    for line in range(z_count):
        block = jnp.transpose(lines[line])
        latents_ref[:, line * 128 : (line + 1) * 128] = block[0:64]
    per_group = VC // GROUPS
    entries = 2 * image_cols * per_group
    row_c = lax.broadcasted_iota(jnp.int32, (VC, VC), 0) // per_group
    col_c = lax.broadcasted_iota(jnp.int32, (VC, VC), 1) // per_group
    same = (row_c == col_c).astype(jnp.float32).astype(jnp.bfloat16)
    wide = dot_exact(sums[...], front[...])
    wide = wide[:, 0:VC] + wide[:, VC : 2 * VC] + wide[:, 2 * VC : 3 * VC] + wide[:, 3 * VC :]
    average = dot_exact(wide, same) / entries
    means[...] = average

    def one_slot(slot, carry):
        patch = patches[slot]
        mean = means[pl.ds(slot, 1), :]
        collected = None
        for out in range(4):
            value = dot32(patch, front[:, out * VC : (out + 1) * VC]) - mean
            value = value * value
            part = value[0:8]
            for at in range(8, tokens, 8):
                part = part + value[at : at + 8]
            collected = part if collected is None else collected + part
        squares[pl.ds(slot, 1), :] = jnp.sum(collected, axis=0, keepdims=True)
        return carry

    lax.fori_loop(0, slots, one_slot, 0)
    variance = dot_exact(squares[...], same) / entries
    spread = lax.rsqrt(variance + EPSILON)
    gain = gain_ref[...]
    count = (tile_tokens + 2) * slots
    row_t = lax.broadcasted_iota(jnp.int32, (count, 1), 0)
    token = row_t // slots
    slot_of = row_t - token * slots
    token = token + mp * tile_tokens - 1
    inside = (token >= 0) & (token < tokens)
    wanted = jnp.where(inside, slot_of * tokens + token, -1)
    column = lax.broadcasted_iota(jnp.int32, (count, slots * tokens), 1)
    pick = (column == wanted).astype(jnp.float32).astype(jnp.bfloat16)
    rows = dot32(pick, patches[...].reshape(slots * tokens, 128)).astype(jnp.bfloat16)
    for out in range(4):
        row_out, col_out = out // 2, out % 2
        value = dot32(rows, front[:, out * VC : (out + 1) * VC])
        for t in range(tile_tokens + 2):
            part = value[t * slots : (t + 1) * slots]
            at = (2 * t + col_out) * slots
            if 1 <= t <= tile_tokens:
                center[row_out, at - 2 * slots : at - slots, :] = part
            scaled = (part - average) * spread * gain
            silu = 0.5 * scaled * (1.0 + jnp.tanh(0.5 * scaled))
            if t == 0:
                silu = jnp.where(mp == 0, 0.0, silu)
            if t == tile_tokens + 1:
                silu = jnp.where(mp == mp_count - 1, 0.0, silu)
            act[row_out, at : at + slots, :] = silu.astype(jnp.bfloat16)
    weight_copy.wait()
    size = tile * slots
    row_p = lax.broadcasted_iota(jnp.int32, (size, size), 0)
    col_p = lax.broadcasted_iota(jnp.int32, (size, size), 1)
    slot_p = row_p // tile
    swap = (col_p == (row_p - slot_p * tile) * slots + slot_p).astype(jnp.float32)
    swap = swap.astype(jnp.bfloat16)
    for row_out in range(2):
        total = center[row_out]
        for row_in in range(2):
            for shift in range(3):
                at = (1 + shift) * slots
                total = total + dot32(
                    act[row_in, at : at + size, :], conv_mid_ref[row_in - row_out + 1, shift]
                )
        ordered = dot32(swap, total.astype(jnp.bfloat16)).astype(jnp.bfloat16)
        out_ref[:, row_out, :, :] = ordered.reshape(slots, tile, VC)


def per_device_fast(
    noise_init,
    step_noise,
    assign,
    slot_map,
    prompt_embed,
    time_vec,
    w_in,
    ln_gain,
    w_up,
    w_down,
    w_out,
    conv_in_w,
    gn_gain,
    conv_mid_w,
):
    segments = lax.axis_size("segment")
    mp_count = lax.axis_size("mp")
    around = range(1, segments)
    along = range(2, mp_count, 2)
    width = w_in.shape[1]
    features = width * mp_count
    latent = w_in.shape[0] * segments
    prompts = prompt_embed.shape[0] * segments
    samples_here = assign.shape[0]
    tok_group = noise_init.shape[0]
    tokens = tok_group // mp_count
    hidden = w_up.shape[1]
    quarter = hidden // segments
    bf16, f32 = jnp.bfloat16, jnp.float32
    any_space = pl.BlockSpec(memory_space=pl.ANY)
    smem = pl.BlockSpec(memory_space=pltpu.SMEM)
    joint = w_up.shape[0] * 3 // 2 + quarter * (w_down.shape[1] // 128)
    pack, *split = pl.pallas_call(
        functools.partial(split_kernel, (segments, quarter)),
        out_shape=[jax.ShapeDtypeStruct((ROWS, width), bf16)]
        + [jax.ShapeDtypeStruct((joint, 128), bf16)] * segments,
        in_specs=whole(7),
        out_specs=whole(1 + segments),
        name="split_weights",
    )(w_in, w_out.T, prompt_embed, time_vec, ln_gain, w_up, w_down)
    table = jnp.stack([pack] + xor_pieces(pack, "segment", around))
    sources = [split[0]]
    for other in around:
        sources += xor_pieces(split[other], "segment", [other])
    table = jnp.stack([table] + xor_pieces(table, "mp", along))
    (table_other,) = xor_pieces(table, "mp", [1])
    scaled, tables, w_out_all = pl.pallas_call(
        functools.partial(table_kernel, (segments, features, mp_count, latent, prompts)),
        out_shape=[
            jax.ShapeDtypeStruct((mp_count, 256, width), bf16),
            jax.ShapeDtypeStruct((mp_count, 128, width), bf16),
            jax.ShapeDtypeStruct((features, 128), bf16),
        ],
        in_specs=[any_space] * 2,
        out_specs=whole(3),
        scratch_shapes=[
            pltpu.VMEM(table.shape, bf16),
            pltpu.VMEM(table.shape, bf16),
            pltpu.VMEM((mp_count, 128, width), f32),
            pltpu.SemaphoreType.DMA((2,)),
        ],
        compiler_params=pltpu.CompilerParams(vmem_limit_bytes=16 * MIB),
        name="order_tables",
    )(table, table_other)
    piece = pl.pallas_call(
        functools.partial(combine_kernel, (segments, mp_count, width, quarter)),
        out_shape=jax.ShapeDtypeStruct((quarter + 32, 128), bf16),
        in_specs=whole(2) + [any_space] * segments,
        out_specs=whole(1)[0],
        scratch_shapes=[
            pltpu.VMEM((segments, joint, 128), bf16),
            pltpu.SemaphoreType.DMA((segments,)),
        ],
        compiler_params=pltpu.CompilerParams(vmem_limit_bytes=16 * MIB),
        name="combine_weights",
    )(scaled, w_out_all, *sources)
    line = jnp.stack([piece] + xor_pieces(piece, "mp", along))
    plane = [line]
    for other in around:
        plane += xor_pieces(line, "segment", [other])
    plane = plane + [xor_pieces(block, "mp", [1])[0] for block in plane]
    half = mp_count // 2
    moments = pl.pallas_call(
        functools.partial(moment_kernel, features),
        out_shape=jax.ShapeDtypeStruct((128, 640), bf16),
        in_specs=whole(2),
        out_specs=whole(1)[0],
        compiler_params=pltpu.CompilerParams(vmem_limit_bytes=8 * MIB),
        name="moments",
    )(tables, w_out_all)
    result = pl.pallas_call(
        functools.partial(loop_kernel, (features, prompts)),
        out_shape=jax.ShapeDtypeStruct((tokens // 2, 128), f32),
        in_specs=[smem] + whole(3) + [any_space] * len(plane),
        out_specs=whole(1)[0],
        scratch_shapes=[
            pltpu.VMEM((tokens, 128), f32),
            pltpu.VMEM((STEPS, tokens, 128), f32),
            pltpu.VMEM((80, len(plane) * half * quarter), bf16),
            pltpu.VMEM((len(plane) * half * quarter // 2, 128), bf16),
            pltpu.VMEM((len(plane), half, 48, 128), bf16),
            pltpu.VMEM((len(plane), half, 96, 128), bf16),
            pltpu.VMEM((128, 64), f32),
            pltpu.SemaphoreType.DMA((len(plane), half + 2)),
        ],
        compiler_params=pltpu.CompilerParams(vmem_limit_bytes=24 * MIB),
        name="denoise",
    )(assign, noise_init.T, step_noise.transpose(0, 2, 1), moments, *plane)
    image = jnp.stack([result] + xor_pieces(result, "mp", along))
    image = jnp.concatenate([image] + xor_pieces(image, "segment", around), axis=0)
    (image_other,) = xor_pieces(image, "mp", [1])
    image_cols = 2 * tokens
    tile = image_cols // mp_count
    slots = 2 * samples_here
    pieces = segments * mp_count
    latents, decoded = pl.pallas_call(
        functools.partial(decode_kernel, (segments, mp_count, samples_here, image_cols)),
        out_shape=[
            jax.ShapeDtypeStruct((64, tok_group), f32),
            jax.ShapeDtypeStruct((slots, 2, tile, VC), bf16),
        ],
        in_specs=[smem, any_space, any_space] + whole(2) + [any_space],
        out_specs=whole(2),
        scratch_shapes=[
            pltpu.SMEM((slots,), jnp.int32),
            pltpu.VMEM((pieces + 1, tokens // 2, 128), f32),
            pltpu.VMEM((slots, tokens, 128), bf16),
            pltpu.VMEM((128, 4 * VC), bf16),
            pltpu.VMEM((slots, 128), f32),
            pltpu.VMEM((slots, VC), f32),
            pltpu.VMEM((slots, VC), f32),
            pltpu.VMEM((2, (tile + 4) * slots, VC), bf16),
            pltpu.VMEM((2, tile * slots, VC), f32),
            pltpu.VMEM((half, 128, 128), f32),
            pltpu.VMEM(conv_mid_w.shape, bf16),
            pltpu.SemaphoreType.DMA((3,)),
        ],
        compiler_params=pltpu.CompilerParams(vmem_limit_bytes=40 * MIB),
        name="decode",
    )(slot_map, image, image_other, conv_in_w, gn_gain[None, :], conv_mid_w)
    return latents.T, decoded


def choose(*args):
    segments, mp_count = lax.axis_size("segment"), lax.axis_size("mp")
    noise, assign, prompt, w_in, w_up = (args[i].shape for i in (0, 2, 4, 6, 8))
    ready = (
        mp_count == 2 * segments == 8
        and noise[0] // mp_count == noise[0] // assign[0] == 64
        and w_up[1] // segments == w_in[1] == 192
        and w_in[0] * segments == noise[1] == 64
        and prompt[0] * segments <= 8
    )
    return (per_device_fast if ready else per_device)(*args)


def solution(mesh):
    return jax.shard_map(
        choose,
        mesh=mesh,
        in_specs=(
            P("segment", None),
            P(None, "segment", None),
            P("segment"),
            P(),
            P("segment", "mp"),
            P("mp"),
            P("segment", "mp"),
            P("mp"),
            P("segment", "mp"),
            P("mp", "segment"),
            P("mp", "segment"),
            P(),
            P(),
            P(),
        ),
        out_specs=(P("segment", None), P("segment", None, "mp", None)),
        check_vma=False,
    )
```
